32 devices in a mesh: tm: 4 (over z), space: 2 (over y), clip: 4 (over x, core).
Axes of the slice: x: 2, y: 2, z: 4, core: 2. Of those that a mesh axis runs over, the one named last changes fastest.
Arguments:
- activations: bfloat16 [96, 64, 1408], P(('clip', 'tm'), 'space'), parts along dimension 0, may hold values from -200 to 200
- attn_gain: float32 [1408], replicated, may hold values from 0.5 to 2
- attn_shift: float32 [1408], replicated, may hold values from -3 to 3
- w_qkv: bfloat16 [1408, 4224], replicated, may hold values from -4 to 4
- b_qkv: float32 [4224], replicated, may hold values from -3 to 3
- w_out: bfloat16 [1408, 1408], replicated, may hold values from -2.5 to 2.5
- b_out: float32 [1408], replicated, may hold values from -3 to 3
- final_gain: float32 [1408], replicated, may hold values from 0.5 to 2
- final_shift: float32 [1408], replicated, may hold values from -3 to 3
- mask_tokens: int32 [32, 192], P('clip'), parts along dimension 0, may hold values from -1 to 1535, as said below
- assignment: int32 [32], P('clip'), parts along dimension 0, may hold values from 0 to 7, each once
Outputs:
- targets: bfloat16 [32, 192, 1408], P(('clip', 'tm', 'space')), parts along dimension 0
The draws below stay inside these ranges and needn't reach their ends.
There are 4 independent parts, one for each index of `clip`. The reference program is written for one: setup_inputs(seed, part) draws one part's arguments, and reference() takes and returns one part's arrays. A program takes and returns all parts, laid end to end along the dimension named above; an argument that names none is the same for every part. Nothing has to cross between parts.
Inputs may be any that keep to these rules, and one draw needn't show every extreme that they name: `mask_tokens`: each row lists distinct tokens, no token in two rows; its listed entries come first in no fixed order, then -1 to the end. The block of tokens of one device (temporal positions k * 6 to k * 6 + 5 and patch positions m * 32 to m * 32 + 31) gives at most 24 entries to one row; in some row every such block gives exactly 24, so that row is full. `assignment`: each owner once.
All inputs are finite; a program needn't handle non-finite values.
Results may differ from the reference program's by a relative error of at most 0.0085.
The reference program's roundings to bfloat16 on the way (of `normed_in`, `projected`, `rounded`, `attended`, `hidden` and `normed`) count: a program that leaves them out, or rounds other values in their place, can miss the bound.
Values may be sent and summed in bfloat16 or wider, within the bound.
A program may use at most 128 MiB of HBM per device.

```python
import math
import jax
import jax.numpy as jnp
from jax import lax

D = 1408
HEADS = 16
HD = 88
T_DEV = 6
S_DEV = 32
TEMPORAL = 24
SPATIAL = 64
TOK_DEV = 192
TOKENS = 1536
OWNERS = 8
SRC_CAP = 24
CAP = 192


def draw_activations(key, part):
    noise_key = jax.random.fold_in(key, 0)
    drawn = jnp.clip(jax.random.normal(noise_key, (TOKENS, D), jnp.float32), -6.0, 6.0)
    return drawn.reshape(TEMPORAL, SPATIAL, D).astype(jnp.bfloat16)


def draw_w_qkv(key, part):
    second_key = jax.random.fold_in(key, 1)
    third_key = jax.random.fold_in(key, 2)
    query_key_part = jnp.clip(jax.random.normal(second_key, (D, 2 * D), jnp.float32), -6.0, 6.0) * math.sqrt(1.5 / D)
    value_part = jnp.clip(jax.random.normal(third_key, (D, D), jnp.float32), -6.0, 6.0) / math.sqrt(D)
    return jnp.concatenate((query_key_part, value_part), axis=1).astype(jnp.bfloat16)


def pick_order(source_seed):
    return jax.random.permutation(source_seed, TOK_DEV)


def pick_rank(owner_seed):
    return jax.random.permutation(owner_seed, CAP)


def draw_mask_tokens(key, part):
    count_key, full_key, source_key, order_key = jax.random.split(key, 4)
    spaces = SPATIAL // S_DEV
    counts = jax.random.randint(count_key, (OWNERS, OWNERS), 0, SRC_CAP + 1)
    full_owner = jax.random.randint(full_key, (), 0, OWNERS)
    counts = jnp.where(jnp.arange(OWNERS)[:, None] == full_owner, SRC_CAP, counts)
    starts = jnp.cumsum(counts, axis=0) - counts
    orders = jax.vmap(pick_order)(jax.random.split(source_key, OWNERS))
    slots = jnp.arange(SRC_CAP)
    positions = jnp.minimum(starts[:, :, None] + slots[None, None, :], TOK_DEV - 1)
    sources = jnp.broadcast_to(jnp.arange(OWNERS)[None, :, None], positions.shape)
    local_rows = orders[sources, positions]
    frames = sources // spaces * T_DEV + local_rows // S_DEV
    patches = sources % spaces * S_DEV + local_rows % S_DEV
    token_ids = (frames * SPATIAL + patches).reshape(OWNERS, CAP)
    listed = (slots[None, None, :] < counts[:, :, None]).reshape(OWNERS, CAP)
    ranks = jax.vmap(pick_rank)(jax.random.split(order_key, OWNERS))
    sort_keys = jnp.where(listed, ranks, CAP + jnp.arange(CAP)[None, :])
    new_order = jnp.argsort(sort_keys, axis=1, stable=True)
    token_ids = jnp.take_along_axis(token_ids, new_order, axis=1)
    listed = jnp.take_along_axis(listed, new_order, axis=1)
    return jnp.where(listed, token_ids, -1).astype(jnp.int32)


def scatter_about(stream_key, dims, scale, most, dtype=jnp.bfloat16):
    result = jax.random.normal(stream_key, dims, jnp.float32) * scale
    return jnp.minimum(jnp.maximum(result, -most), most).astype(dtype)


def setup_inputs(seed: int = 0, part: int = 0) -> dict:
    splits = jax.random.split(jax.random.key(seed), 12)
    own_keys = jax.random.split(jax.random.fold_in(splits[11], part), 12)
    return {
        "activations": draw_activations(jax.random.fold_in(jax.random.fold_in(splits[11], part), 71), part),
        "attn_gain": jnp.clip(jnp.exp(jax.random.uniform(splits[1], (D,), jnp.float32, math.log(0.5), math.log(2.0))), 0.5, 2.0),
        "attn_shift": scatter_about(splits[2], (D,), 0.5, 3.0, jnp.float32),
        "w_qkv": draw_w_qkv(jax.random.fold_in(splits[11], 71), part),
        "b_qkv": scatter_about(splits[4], (3 * D,), 0.5, 3.0, jnp.float32),
        "w_out": scatter_about(splits[5], (D, D), (max(D // 256, 1)) ** -0.5, 2.5),
        "b_out": scatter_about(splits[6], (D,), 0.5, 3.0, jnp.float32),
        "final_gain": jnp.clip(jnp.exp(jax.random.uniform(splits[7], (D,), jnp.float32, math.log(0.5), math.log(2.0))), 0.5, 2.0),
        "final_shift": scatter_about(splits[8], (D,), 0.5, 3.0, jnp.float32),
        "mask_tokens": draw_mask_tokens(jax.random.fold_in(jax.random.fold_in(splits[11], part), 71), part),
        "assignment": jax.random.permutation(own_keys[10], OWNERS).astype(jnp.int32),
    }


EPSILON = 1e-06

def layer_norm(values, ln_gain, ln_shift):
    centre = lax.optimization_barrier(jnp.mean(values, axis=-1, keepdims=True))
    deviation = values - centre
    variance = lax.optimization_barrier(jnp.mean(deviation * deviation, axis=-1, keepdims=True))
    return deviation * lax.rsqrt(variance + EPSILON) * ln_gain + ln_shift

def reference(activations, attn_gain, attn_shift, w_qkv, b_qkv, w_out, b_out, final_gain, final_shift, mask_tokens, assignment):
    tokens_flat = activations.reshape(TOKENS, D)
    normed_in = layer_norm(tokens_flat.astype(jnp.float32), attn_gain, attn_shift).astype(jnp.bfloat16)
    projected = (jnp.dot(normed_in, w_qkv, preferred_element_type=jnp.float32) + b_qkv).astype(jnp.bfloat16)
    query_blocks = projected[:, :D].reshape(TOKENS // TOK_DEV, TOK_DEV, HEADS, HD)
    key_rows = projected[:, D:2 * D].reshape(TOKENS, HEADS, HD).astype(jnp.float32)
    value_rows = projected[:, 2 * D:].reshape(TOKENS, HEADS, HD).astype(jnp.float32)
    score_scale = 1.0 / math.sqrt(HD)

    def attend_block(query_block):
        scores = jnp.einsum('qhe,khe->hqk', query_block.astype(jnp.float32), key_rows) * score_scale
        highest = lax.optimization_barrier(jnp.max(scores, axis=-1, keepdims=True))
        weights = jnp.exp(scores - highest)
        totals = lax.optimization_barrier(jnp.sum(weights, axis=-1))
        rounded = lax.optimization_barrier(weights.astype(jnp.bfloat16))
        weighted = jnp.einsum('hqk,khe->hqe', rounded.astype(jnp.float32), value_rows)
        return jnp.transpose(weighted / totals[:, :, None], (1, 0, 2)).astype(jnp.bfloat16)
    attended = lax.map(attend_block, query_blocks).reshape(TOKENS, D)
    projected_out = jnp.dot(attended, w_out, preferred_element_type=jnp.float32)
    hidden = (tokens_flat.astype(jnp.float32) + projected_out + b_out).astype(jnp.bfloat16)
    normed = layer_norm(hidden.astype(jnp.float32), final_gain, final_shift).astype(jnp.bfloat16)
    owner_lists = jnp.take(mask_tokens, assignment, axis=0)
    picked = jnp.take(normed, jnp.maximum(owner_lists, 0), axis=0)
    return jnp.where((owner_lists >= 0)[:, :, None], picked, jnp.zeros_like(picked))
```

```python
import functools
import math

import jax
import jax.numpy as jnp
import numpy as np
from jax import lax
from jax.experimental import pallas as pl
from jax.experimental.pallas import tpu as pltpu
from jax.sharding import PartitionSpec as P

HEADS = 16


EPSILON = 1e-06
FLOOR_SCORE = -1e30


def layer_norm(values, ln_gain, ln_shift):
    centre = jnp.mean(values, axis=-1, keepdims=True)
    deviation = values - centre
    variance = jnp.mean(deviation * deviation, axis=-1, keepdims=True)
    return deviation * lax.rsqrt(variance + EPSILON) * ln_gain + ln_shift


def start_state(query_heads):
    query_count, head_count, head_width = query_heads.shape
    return (
        jnp.full((head_count, query_count), FLOOR_SCORE, jnp.float32),
        jnp.zeros((head_count, query_count), jnp.float32),
        jnp.zeros((head_count, query_count, head_width), jnp.float32),
    )


def finish_state(carried_state):
    running_max, running_total, running_sum = carried_state
    return jnp.transpose(running_sum / running_total[:, :, None], (1, 0, 2)).astype(jnp.bfloat16)


def make_attend(query_heads):
    query_count, head_count, head_width = query_heads.shape
    score_scale = 1.0 / math.sqrt(head_width)

    def one_block(carried_state, kv_block):
        running_max, running_total, running_sum = carried_state
        block_length = kv_block.shape[1]
        key_rows = kv_block[0].reshape(block_length, head_count, head_width)
        value_rows = kv_block[1].reshape(block_length, head_count, head_width)
        scores = (
            jnp.einsum("qhe,khe->hqk", query_heads, key_rows, preferred_element_type=jnp.float32)
            * score_scale
        )
        new_max = jnp.maximum(running_max, jnp.max(scores, axis=-1))
        factor = jnp.exp(running_max - new_max)
        weights = jnp.exp(scores - new_max[:, :, None])
        running_total = running_total * factor + jnp.sum(weights, axis=-1)
        running_sum = running_sum * factor[:, :, None] + jnp.einsum(
            "hqk,khe->hqe",
            weights.astype(jnp.bfloat16),
            value_rows,
            preferred_element_type=jnp.float32,
        )
        return (new_max, running_total, running_sum)

    def attend(carried_state, key_piece, first_row):
        length = key_piece.shape[1]
        block_rows = length
        while block_rows > 1024 and block_rows % 2 == 0:
            block_rows = block_rows // 2

        def advance(position, carried):
            kv_block = lax.dynamic_slice_in_dim(key_piece, position * block_rows, block_rows, 1)
            return one_block(carried, kv_block)

        return lax.fori_loop(0, length // block_rows, advance, carried_state)

    return attend


def local(
    activations,
    attn_gain,
    attn_shift,
    w_qkv,
    b_qkv,
    w_out,
    b_out,
    final_gain,
    final_shift,
    mask_tokens,
    assignment,
):
    frame_count, patch_count, model_width = activations.shape
    local_rows = frame_count * patch_count
    head_width = model_width // HEADS
    tokens_flat = activations.reshape(local_rows, model_width)
    normed_in = layer_norm(tokens_flat.astype(jnp.float32), attn_gain, attn_shift).astype(
        jnp.bfloat16
    )
    projected = (jnp.dot(normed_in, w_qkv, preferred_element_type=jnp.float32) + b_qkv).astype(
        jnp.bfloat16
    )
    query_rows = projected[:, :model_width]
    paired = jnp.stack(
        (projected[:, model_width : 2 * model_width], projected[:, 2 * model_width :])
    )
    groups = lax.axis_size("space")
    group_heads = HEADS // groups
    stacked = jnp.stack((query_rows, paired[0], paired[1])).reshape(
        3, local_rows, groups, group_heads, head_width
    )
    swapped = lax.all_to_all(stacked, "space", split_axis=2, concat_axis=1, tiled=True)
    gathered_rows = swapped.shape[1]
    kept_heads = swapped.shape[3]
    query_heads = swapped[0].reshape(gathered_rows, kept_heads, head_width)
    kv_rows = swapped[1:].reshape(2, gathered_rows, kept_heads * head_width)
    time_state = make_attend(query_heads)(
        start_state(query_heads), lax.all_gather(kv_rows, "tm", axis=1, tiled=True), jnp.int32(0)
    )
    head_output = finish_state(time_state).reshape(gathered_rows, 1, kept_heads, head_width)
    merged = lax.all_to_all(head_output, "space", split_axis=0, concat_axis=1, tiled=True)
    attended = merged.reshape(local_rows, model_width)
    hidden = (
        tokens_flat.astype(jnp.float32)
        + jnp.dot(attended, w_out, preferred_element_type=jnp.float32)
        + b_out
    ).astype(jnp.bfloat16)
    normed = layer_norm(hidden.astype(jnp.float32), final_gain, final_shift).astype(jnp.bfloat16)
    owners = mask_tokens.shape[0]
    capacity = mask_tokens.shape[1]
    per_source = capacity // owners
    spaces = lax.axis_size("space")
    spatial = patch_count * spaces
    own_index = lax.axis_index("tm") * spaces + lax.axis_index("space")
    owner_lists = jnp.take(mask_tokens, assignment, axis=0)
    listed = owner_lists >= 0
    clipped = jnp.maximum(owner_lists, 0)
    token_frame = clipped // spatial
    token_patch = clipped % spatial
    home_device = token_frame // frame_count * spaces + token_patch // patch_count
    local_row = token_frame % frame_count * patch_count + token_patch % patch_count
    mine = listed & (home_device == own_index)
    slot_index = jnp.cumsum(mine.astype(jnp.int32), axis=1) - 1
    wanted = mine[:, None, :] & (
        slot_index[:, None, :] == jnp.arange(per_source, dtype=jnp.int32)[None, :, None]
    )
    picks = jnp.sum(jnp.where(wanted, local_row[:, None, :], 0), axis=-1)
    present = jnp.any(wanted, axis=-1)
    own_home = lax.dynamic_index_in_dim(home_device, own_index, 0, keepdims=False)
    own_listed = lax.dynamic_index_in_dim(listed, own_index, 0, keepdims=False)
    entry_order = jnp.arange(capacity, dtype=jnp.int32)
    earlier = (
        (entry_order[:, None] < entry_order[None, :])
        & own_listed[:, None]
        & (own_home[:, None] == own_home[None, :])
    )
    entry_rank = jnp.sum(earlier.astype(jnp.int32), axis=0)
    where_from = jnp.where(own_listed, own_home * per_source + entry_rank, 0)
    outgoing = jnp.where(
        present[:, :, None], jnp.take(normed, picks, axis=0), jnp.zeros((), jnp.bfloat16)
    )
    arrived = lax.all_to_all(outgoing, ("tm", "space"), split_axis=0, concat_axis=0, tiled=True)
    row_table = arrived.reshape(owners * per_source, model_width)
    placed = jnp.take(row_table, where_from, axis=0)
    return jnp.where(own_listed[:, None], placed, jnp.zeros((), jnp.bfloat16))[None]


LANES = 128
WINDOW = 256
VMEM_LIMIT = 60 * 1024 * 1024
MESH = pl.DeviceIdType.MESH


def norm_rows(values, gain, shift):
    return layer_norm(values.astype(jnp.float32), gain, shift).astype(jnp.bfloat16)


def fused_kernel(
    times,
    head_width,
    x_ref,
    gain_flat,
    shift_flat,
    w_qkv_ref,
    b_qkv_flat,
    w_out_ref,
    b_out_flat,
    final_gain_flat,
    final_shift_flat,
    lists_ref,
    assignment_ref,
    columns_ref,
    out_ref,
    x_all,
    kv_all,
    w_qkv,
    w_out,
    normed,
    queries,
    attended,
    b_qkv_ref,
    vectors,
    local_sem,
    up_send,
    down_send,
    side_send,
    line_recv,
    side_recv,
    mate_sem,
):
    me = lax.axis_index("tm")
    side = lax.axis_index("space")
    other = 1 - side
    rows, width = x_ref.shape
    half_rows = rows // 2
    mate = me + 1 - 2 * lax.rem(me, 2)
    load_x = [
        pltpu.make_async_copy(
            x_ref.at[pl.ds(half * half_rows, half_rows)],
            x_all.at[me, side, half],
            local_sem.at[2 + half],
        )
        for half in range(2)
    ]
    load_qkv = pltpu.make_async_copy(w_qkv_ref, w_qkv, local_sem.at[0])
    load_out = pltpu.make_async_copy(w_out_ref, w_out, local_sem.at[1])
    for load in load_x:
        load.start()
    load_qkv.start()
    load_out.start()

    has_up = me < times - 1
    has_down = me > 0

    barrier = pltpu.get_barrier_semaphore()
    pl.semaphore_signal(barrier, inc=1, device_id={"space": other}, device_id_type=MESH)

    @pl.when(has_up)
    def _():
        pl.semaphore_signal(barrier, inc=1, device_id={"tm": me + 1}, device_id_type=MESH)

    @pl.when(has_down)
    def _():
        pl.semaphore_signal(barrier, inc=1, device_id={"tm": me - 1}, device_id_type=MESH)

    pl.semaphore_wait(barrier, 1 + has_up.astype(jnp.int32) + has_down.astype(jnp.int32))

    def up_copy(source, block, half):
        return pltpu.make_async_remote_copy(
            source, x_all.at[block, side, half], up_send.at[block, half],
            line_recv.at[block, half], device_id={"tm": me + 1}, device_id_type=MESH,
        )

    def down_copy(source, block, half):
        return pltpu.make_async_remote_copy(
            source, x_all.at[block, side, half], down_send.at[block, half],
            line_recv.at[block, half], device_id={"tm": me - 1}, device_id_type=MESH,
        )

    def side_copy(block, half, from_side, source=None):
        place = x_all.at[block, from_side, half]
        return pltpu.make_async_remote_copy(
            place if source is None else source, place, side_send.at[block, half],
            side_recv.at[block, half], device_id={"space": other}, device_id_type=MESH,
        )

    def mate_copy(block):
        place = x_all.at[block, other, 1]
        return pltpu.make_async_remote_copy(
            place, place, mate_sem.at[0], mate_sem.at[1],
            device_id={"tm": mate}, device_id_type=MESH,
        )

    for half in range(2):
        own_half = x_ref.at[pl.ds(half * half_rows, half_rows)]

        @pl.when(has_up)
        def _():
            up_copy(own_half, me, half).start()

        @pl.when(has_down)
        def _():
            down_copy(own_half, me, half).start()

        side_copy(me, half, side, own_half).start()

    b_qkv_ref[...] = b_qkv_flat[...].reshape(1, 3 * width)
    flats = (gain_flat, shift_flat, b_out_flat, final_gain_flat, final_shift_flat)
    for place, flat in enumerate(flats):
        vectors[place : place + 1, :] = flat[...].reshape(1, width)
    gain_ref, shift_ref, b_out_ref, final_gain_ref, final_shift_ref = (
        vectors.at[place : place + 1, :] for place in range(len(flats))
    )

    def send_aside(block, half):
        if half == 0:
            side_copy(block, half, side).start()
        else:

            @pl.when(block != mate)
            def _():
                side_copy(block, half, side).start()

    def arrive_and_forward(step, half):
        below, above = me - step, me + step

        @pl.when(below >= 0)
        def _():
            held = x_all.at[below, side, half]
            up_copy(held, below, half).wait_recv()

            @pl.when(has_up)
            def _():
                up_copy(held, below, half).start()

            send_aside(below, half)

        @pl.when(above < times)
        def _():
            held = x_all.at[above, side, half]
            down_copy(held, above, half).wait_recv()

            @pl.when(has_down)
            def _():
                down_copy(held, above, half).start()

            send_aside(above, half)

    reach = jnp.minimum(me, times - 1 - me)
    toward = mate - me

    def ordered(place):
        if place == 0:
            return me
        near = me + ((place + 1) // 2) * (toward if place % 2 else -toward)
        far_step = place - reach
        far = jnp.where(2 * me > times - 1, me - far_step, me + far_step)
        return jnp.where(place <= 2 * reach, near, far)

    tiles = 2

    def project(pieces):
        count = len(pieces)
        for place, (block, from_side, half) in enumerate(pieces):
            normed[place * half_rows : (place + 1) * half_rows, :] = norm_rows(
                x_all[block, from_side, half], gain_ref[...], shift_ref[...]
            )

        def one_tile(tile, carried):
            start = pl.multiple_of(tile * width, LANES)
            shifted = pl.multiple_of(width + tile * width, LANES)
            made = jnp.dot(
                normed[: count * half_rows, :],
                w_qkv[:, pl.ds(shifted, width)],
                preferred_element_type=jnp.float32,
            )
            made = (made + b_qkv_ref[:, pl.ds(shifted, width)]).astype(jnp.bfloat16)
            for place, (block, from_side, half) in enumerate(pieces):
                kv_all[block * 2 + from_side, half, :, pl.ds(start, width)] = made[
                    place * half_rows : (place + 1) * half_rows, :
                ]
            return carried

        lax.fori_loop(0, tiles, one_tile, 0)

    def from_aside(place):
        block = ordered(place)
        pieces = []
        for half in range(1 if place == 1 else 2):
            side_copy(block, half, other).wait_recv()
            pieces.append((block, other, half))
        return pieces

    for load in load_x:
        load.wait()
    load_qkv.wait()
    project([(me, side, 0), (me, side, 1)])
    last = ordered(times - 1)
    for step in range(1, times - 1):
        arrive_and_forward(step, 0)
        arrive_and_forward(step, 1)
        ready = from_aside(step - 1)
        if step == times - 2:
            mate_copy(me).start()
        project([(ordered(step), side, 0), (ordered(step), side, 1)] + ready)
    arrive_and_forward(times - 1, 0)
    project([(last, side, 0)] + from_aside(times - 2))
    arrive_and_forward(times - 1, 1)
    side_copy(last, 0, other).wait_recv()
    project([(last, side, 1), (last, other, 0)])
    owner = assignment_ref[me * 2 + side]
    list_places = lax.broadcasted_iota(jnp.int32, lists_ref.shape, 0)
    lists = lists_ref[...].astype(jnp.float32)
    token_row = jnp.sum(jnp.where(list_places == owner, lists, 0.0), axis=0, keepdims=True)
    capacity = lists_ref.shape[1]
    diagonal = lax.broadcasted_iota(jnp.int32, (capacity, capacity), 0) == lax.broadcasted_iota(
        jnp.int32, (capacity, capacity), 1
    )
    tokens = jnp.sum(jnp.where(diagonal, token_row, 0.0), axis=1, keepdims=True)

    def pick(block, from_side):
        listed = tokens == columns_ref[pl.ds(block * 2 + from_side, 1), :]
        return jnp.dot(
            listed.astype(jnp.float32).astype(jnp.bfloat16),
            x_all[block, from_side].reshape(rows, width),
            preferred_element_type=jnp.float32,
        )

    picked = pick(0, side)
    for block in range(1, times):
        picked += pick(block, side)

    side_copy(last, 1, other).wait_recv()
    mate_copy(mate).wait_recv()
    project([(last, other, 1), (mate, other, 1)])

    for block in range(times):
        picked += pick(block, other)
    out_ref[0] = picked.astype(jnp.bfloat16)
    queries[...] = (
        jnp.dot(
            norm_rows(picked, gain_ref[...], shift_ref[...]),
            w_qkv[:, :width],
            preferred_element_type=jnp.float32,
        )
        + b_qkv_ref[:, :width]
    ).astype(jnp.bfloat16)
    attended[...] = jnp.zeros_like(attended)
    score_scale = math.log2(math.e) / math.sqrt(head_width)
    all_rows = times * 2 * rows

    def window_of(first):
        return min(first // LANES, width // LANES - 2) * LANES

    groups = []
    head = 0
    while head < HEADS:
        base = window_of(head * head_width)
        count = 1
        while head + count < HEADS and (head + count + 1) * head_width <= base + WINDOW:
            count += 1
        groups.append((base, range(head, head + count)))
        head += count

    for base, heads in groups:
        lane = lax.broadcasted_iota(jnp.int32, (capacity, WINDOW), 1) + base
        inside = [(lane >= h * head_width) & (lane < (h + 1) * head_width) for h in heads]
        window_queries = queries[:, base : base + WINDOW].astype(jnp.float32)
        query = jnp.concatenate(
            [jnp.where(mask, window_queries, 0.0).astype(jnp.bfloat16) for mask in inside]
        )
        keys = kv_all[:, :, :, base : base + WINDOW].reshape(all_rows, WINDOW)
        values = kv_all[:, :, :, width + base : width + base + WINDOW].reshape(all_rows, WINDOW)
        scores = (
            lax.dot_general(
                query, keys, (((1,), (1,)), ((), ())), preferred_element_type=jnp.float32
            )
            * score_scale
        )
        weights = jnp.exp2(scores - jnp.max(scores, axis=1, keepdims=True))
        totals = jnp.sum(weights, axis=1, keepdims=True)
        summed = jnp.dot(weights.astype(jnp.bfloat16), values, preferred_element_type=jnp.float32)
        summed = summed / totals
        for place, mask in enumerate(inside):
            attended[:, base : base + WINDOW] += jnp.where(
                mask, summed[place * capacity : (place + 1) * capacity], 0.0
            )

    load_out.wait()
    hidden = (
        out_ref[0].astype(jnp.float32)
        + jnp.dot(
            attended[...].astype(jnp.bfloat16), w_out[...], preferred_element_type=jnp.float32
        )
        + b_out_ref[...]
    ).astype(jnp.bfloat16)
    final = layer_norm(hidden.astype(jnp.float32), final_gain_ref[...], final_shift_ref[...])
    out_ref[0] = jnp.where(tokens >= 0, final, 0.0).astype(jnp.bfloat16)

    for block in range(times):
        for half in range(2):

            @pl.when(has_up & (block <= me))
            def _():
                up_copy(x_all.at[block, side, half], block, half).wait_send()

            @pl.when(has_down & (block >= me))
            def _():
                down_copy(x_all.at[block, side, half], block, half).wait_send()

            @pl.when((block != mate) | (half == 0))
            def _():
                side_copy(block, half, side).wait_send()

    mate_copy(me).wait_send()


def fits_fused(times, spaces, rows, width, capacity):
    all_rows = times * spaces * rows
    held = 2 * (all_rows * width * 3 + width * width * 4 + 2 * rows * width)
    held += 4 * capacity * (width * 2 + all_rows * 3)
    return (
        spaces == 2
        and held < VMEM_LIMIT
        and width % LANES == 0
        and width // HEADS <= LANES
        and rows % 32 == 0
        and times % 2 == 0
        and times > 2
    )


def fused_local(
    activations,
    attn_gain,
    attn_shift,
    w_qkv,
    b_qkv,
    w_out,
    b_out,
    final_gain,
    final_shift,
    mask_tokens,
    assignment,
):
    frames, patches, width = activations.shape
    rows = frames * patches
    times = lax.axis_size("tm")
    spaces = lax.axis_size("space")
    if not fits_fused(times, spaces, rows, width, mask_tokens.shape[1]):
        return local(
            activations, attn_gain, attn_shift, w_qkv, b_qkv, w_out, b_out,
            final_gain, final_shift, mask_tokens, assignment,
        )
    capacity = mask_tokens.shape[1]
    order = np.arange(times * frames * spaces * patches).reshape(times, frames, spaces, patches)
    columns = order.transpose(0, 2, 1, 3).reshape(times * spaces, -1).astype(np.float32)
    vmem = pl.BlockSpec(memory_space=pltpu.VMEM)
    hbm = pl.BlockSpec(memory_space=pl.ANY)
    smem = pl.BlockSpec(memory_space=pltpu.SMEM)
    return pl.pallas_call(
        functools.partial(fused_kernel, times, width // HEADS),
        out_shape=jax.ShapeDtypeStruct((1, capacity, width), jnp.bfloat16),
        in_specs=[vmem, vmem, vmem, hbm, vmem, hbm, vmem, vmem, vmem, vmem, smem, vmem],
        out_specs=vmem,
        scratch_shapes=[
            pltpu.VMEM((times, spaces, 2, rows // 2, width), jnp.bfloat16),
            pltpu.VMEM((times * spaces, 2, rows // 2, 2 * width), jnp.bfloat16),
            pltpu.VMEM(w_qkv.shape, jnp.bfloat16),
            pltpu.VMEM(w_out.shape, jnp.bfloat16),
            pltpu.VMEM((2 * rows, width), jnp.bfloat16),
            pltpu.VMEM((capacity, width), jnp.bfloat16),
            pltpu.VMEM((capacity, width), jnp.float32),
            pltpu.VMEM((1, 3 * width), jnp.float32),
            pltpu.VMEM((5, width), jnp.float32),
            pltpu.SemaphoreType.DMA((4,)),
            pltpu.SemaphoreType.DMA((times, 2)),
            pltpu.SemaphoreType.DMA((times, 2)),
            pltpu.SemaphoreType.DMA((times, 2)),
            pltpu.SemaphoreType.DMA((times, 2)),
            pltpu.SemaphoreType.DMA((times, 2)),
            pltpu.SemaphoreType.DMA((2,)),
        ],
        compiler_params=pltpu.CompilerParams(
            collective_id=0, has_side_effects=True, vmem_limit_bytes=VMEM_LIMIT
        ),
    )(
        activations.reshape(rows, width),
        attn_gain,
        attn_shift,
        w_qkv,
        b_qkv,
        w_out,
        b_out,
        final_gain,
        final_shift,
        mask_tokens,
        assignment,
        jnp.asarray(columns),
    )


def solution(mesh):
    in_specs = (
        P(("clip", "tm"), "space", None),
        P(),
        P(),
        P(),
        P(),
        P(),
        P(),
        P(),
        P(),
        P("clip", None),
        P("clip"),
    )
    out_specs = P(("clip", "tm", "space"), None, None)
    return jax.shard_map(fused_local, mesh=mesh, in_specs=in_specs, out_specs=out_specs, check_vma=False)
```

```python
import functools
import math

import jax
import jax.numpy as jnp
from jax import lax
from jax.experimental import pallas as pl
from jax.experimental.pallas import tpu as pltpu
from jax.sharding import PartitionSpec as P

HEADS = 16


EPSILON = 1e-06
FLOOR_SCORE = -1e30


def layer_norm(values, ln_gain, ln_shift):
    centre = jnp.mean(values, axis=-1, keepdims=True)
    deviation = values - centre
    variance = jnp.mean(deviation * deviation, axis=-1, keepdims=True)
    return deviation * lax.rsqrt(variance + EPSILON) * ln_gain + ln_shift


def start_state(query_heads):
    query_count, head_count, head_width = query_heads.shape
    return (
        jnp.full((head_count, query_count), FLOOR_SCORE, jnp.float32),
        jnp.zeros((head_count, query_count), jnp.float32),
        jnp.zeros((head_count, query_count, head_width), jnp.float32),
    )


def finish_state(carried_state):
    running_max, running_total, running_sum = carried_state
    return jnp.transpose(running_sum / running_total[:, :, None], (1, 0, 2)).astype(jnp.bfloat16)


def make_attend(query_heads):
    query_count, head_count, head_width = query_heads.shape
    score_scale = 1.0 / math.sqrt(head_width)

    def one_block(carried_state, kv_block):
        running_max, running_total, running_sum = carried_state
        block_length = kv_block.shape[1]
        key_rows = kv_block[0].reshape(block_length, head_count, head_width)
        value_rows = kv_block[1].reshape(block_length, head_count, head_width)
        scores = (
            jnp.einsum("qhe,khe->hqk", query_heads, key_rows, preferred_element_type=jnp.float32)
            * score_scale
        )
        new_max = jnp.maximum(running_max, jnp.max(scores, axis=-1))
        factor = jnp.exp(running_max - new_max)
        weights = jnp.exp(scores - new_max[:, :, None])
        running_total = running_total * factor + jnp.sum(weights, axis=-1)
        running_sum = running_sum * factor[:, :, None] + jnp.einsum(
            "hqk,khe->hqe",
            weights.astype(jnp.bfloat16),
            value_rows,
            preferred_element_type=jnp.float32,
        )
        return (new_max, running_total, running_sum)

    def attend(carried_state, key_piece, first_row):
        length = key_piece.shape[1]
        block_rows = length
        while block_rows > 1024 and block_rows % 2 == 0:
            block_rows = block_rows // 2

        def advance(position, carried):
            kv_block = lax.dynamic_slice_in_dim(key_piece, position * block_rows, block_rows, 1)
            return one_block(carried, kv_block)

        return lax.fori_loop(0, length // block_rows, advance, carried_state)

    return attend


def local(
    activations,
    attn_gain,
    attn_shift,
    w_qkv,
    b_qkv,
    w_out,
    b_out,
    final_gain,
    final_shift,
    mask_tokens,
    assignment,
):
    frame_count, patch_count, model_width = activations.shape
    local_rows = frame_count * patch_count
    head_width = model_width // HEADS
    tokens_flat = activations.reshape(local_rows, model_width)
    normed_in = layer_norm(tokens_flat.astype(jnp.float32), attn_gain, attn_shift).astype(
        jnp.bfloat16
    )
    projected = (jnp.dot(normed_in, w_qkv, preferred_element_type=jnp.float32) + b_qkv).astype(
        jnp.bfloat16
    )
    query_rows = projected[:, :model_width]
    paired = jnp.stack(
        (projected[:, model_width : 2 * model_width], projected[:, 2 * model_width :])
    )
    groups = lax.axis_size("space")
    group_heads = HEADS // groups
    stacked = jnp.stack((query_rows, paired[0], paired[1])).reshape(
        3, local_rows, groups, group_heads, head_width
    )
    swapped = lax.all_to_all(stacked, "space", split_axis=2, concat_axis=1, tiled=True)
    gathered_rows = swapped.shape[1]
    kept_heads = swapped.shape[3]
    query_heads = swapped[0].reshape(gathered_rows, kept_heads, head_width)
    kv_rows = swapped[1:].reshape(2, gathered_rows, kept_heads * head_width)
    time_state = make_attend(query_heads)(
        start_state(query_heads), lax.all_gather(kv_rows, "tm", axis=1, tiled=True), jnp.int32(0)
    )
    head_output = finish_state(time_state).reshape(gathered_rows, 1, kept_heads, head_width)
    merged = lax.all_to_all(head_output, "space", split_axis=0, concat_axis=1, tiled=True)
    attended = merged.reshape(local_rows, model_width)
    hidden = (
        tokens_flat.astype(jnp.float32)
        + jnp.dot(attended, w_out, preferred_element_type=jnp.float32)
        + b_out
    ).astype(jnp.bfloat16)
    normed = layer_norm(hidden.astype(jnp.float32), final_gain, final_shift).astype(jnp.bfloat16)
    owners = mask_tokens.shape[0]
    capacity = mask_tokens.shape[1]
    per_source = capacity // owners
    spaces = lax.axis_size("space")
    spatial = patch_count * spaces
    own_index = lax.axis_index("tm") * spaces + lax.axis_index("space")
    owner_lists = jnp.take(mask_tokens, assignment, axis=0)
    listed = owner_lists >= 0
    clipped = jnp.maximum(owner_lists, 0)
    token_frame = clipped // spatial
    token_patch = clipped % spatial
    home_device = token_frame // frame_count * spaces + token_patch // patch_count
    local_row = token_frame % frame_count * patch_count + token_patch % patch_count
    mine = listed & (home_device == own_index)
    slot_index = jnp.cumsum(mine.astype(jnp.int32), axis=1) - 1
    wanted = mine[:, None, :] & (
        slot_index[:, None, :] == jnp.arange(per_source, dtype=jnp.int32)[None, :, None]
    )
    picks = jnp.sum(jnp.where(wanted, local_row[:, None, :], 0), axis=-1)
    present = jnp.any(wanted, axis=-1)
    own_home = lax.dynamic_index_in_dim(home_device, own_index, 0, keepdims=False)
    own_listed = lax.dynamic_index_in_dim(listed, own_index, 0, keepdims=False)
    entry_order = jnp.arange(capacity, dtype=jnp.int32)
    earlier = (
        (entry_order[:, None] < entry_order[None, :])
        & own_listed[:, None]
        & (own_home[:, None] == own_home[None, :])
    )
    entry_rank = jnp.sum(earlier.astype(jnp.int32), axis=0)
    where_from = jnp.where(own_listed, own_home * per_source + entry_rank, 0)
    outgoing = jnp.where(
        present[:, :, None], jnp.take(normed, picks, axis=0), jnp.zeros((), jnp.bfloat16)
    )
    arrived = lax.all_to_all(outgoing, ("tm", "space"), split_axis=0, concat_axis=0, tiled=True)
    row_table = arrived.reshape(owners * per_source, model_width)
    placed = jnp.take(row_table, where_from, axis=0)
    return jnp.where(own_listed[:, None], placed, jnp.zeros((), jnp.bfloat16))[None]


LANES = 128
WINDOW = 256
VMEM_LIMIT = 60 * 1024 * 1024
MESH = pl.DeviceIdType.MESH


def norm_rows(values, gain, shift):
    return layer_norm(values.astype(jnp.float32), gain, shift).astype(jnp.bfloat16)


def count_floor(values, size):
    return jnp.floor((values + 0.5) * (1.0 / size))


def small_dot(left, right):
    return jnp.dot(
        left.astype(jnp.bfloat16), right.astype(jnp.bfloat16), preferred_element_type=jnp.float32
    )


def fused_kernel(
    times,
    spaces,
    frames,
    patches,
    head_width,
    x_ref,
    gain_flat,
    shift_flat,
    w_qkv_ref,
    b_qkv_flat,
    w_out_ref,
    b_out_flat,
    final_gain_flat,
    final_shift_flat,
    lists_ref,
    assignment_ref,
    out_ref,
    own,
    x_all,
    k_all,
    v_all,
    w_q,
    w_k,
    w_v,
    w_out,
    normed,
    rows_f32,
    queries,
    sums,
    high,
    total,
    attended,
    attended_in,
    made_rows,
    back_rows,
    unpermute,
    b_qkv_ref,
    vectors,
    load_sem,
    own_sem,
    part_sem,
    side_sem,
    line_sem,
    recv,
    swap_sem,
    back_sem,
):
    me = lax.axis_index("tm")
    side = lax.axis_index("space")
    clip = lax.axis_index("clip")
    core = lax.rem(clip, 2)
    other = 1 - side
    partner = clip + 1 - 2 * core
    mate = me + 1 - 2 * lax.rem(me, 2)
    pair = lax.div(me, 2)
    far = lax.rem(me + 2, times)
    across = times - 1 - me
    active_core = lax.rem(me, 2)
    active = core == active_core
    idle = core != active_core
    inner = (me > 0) & (me < times - 1)
    left = me < times // 2
    rows, width = x_ref.shape
    quarter = rows // 4
    share = quarter // spaces
    owners, capacity = lists_ref.shape
    half_width = width // 2
    first_lane = half_width // LANES * LANES
    span = width - first_lane
    lane_skip = half_width - first_lane

    def core_clip(parity):
        return clip - core + parity

    column = pl.multiple_of(core * first_lane, LANES)
    loads = [
        pltpu.make_async_copy(
            w_qkv_ref.at[:, pl.ds(pl.multiple_of(part * width + column, LANES), span)],
            place,
            load_sem.at[part],
        )
        for part, place in ((1, w_k), (2, w_v), (0, w_q))
    ]
    loads.append(pltpu.make_async_copy(w_out_ref, w_out, load_sem.at[3]))
    for load in loads:
        load.start()

    barrier = pltpu.get_barrier_semaphore()

    def greet(**place):
        pl.semaphore_signal(barrier, inc=1, device_id=place, device_id_type=MESH)

    greet(clip=partner)
    for parity in range(2):
        greet(space=other, clip=core_clip(parity))
        greet(tm=mate, clip=core_clip(parity))
        greet(tm=far, clip=core_clip(parity))

        @pl.when(inner)
        def _():
            greet(tm=across, clip=core_clip(parity))

    b_qkv_ref[...] = b_qkv_flat[...].reshape(1, 3 * width)
    flats = (gain_flat, shift_flat, b_out_flat, final_gain_flat, final_shift_flat)
    for place, flat in enumerate(flats):
        vectors[place : place + 1, :] = flat[...].reshape(1, width)
    gain_ref, shift_ref, b_out_ref, final_gain_ref, final_shift_ref = (
        vectors.at[place : place + 1, :] for place in range(len(flats))
    )

    lists = lists_ref[...].astype(jnp.float32)
    list_places = lax.broadcasted_iota(jnp.int32, lists.shape, 0)

    def list_of(device):
        owner = assignment_ref[device]
        return jnp.sum(jnp.where(list_places == owner, lists, 0.0), axis=0, keepdims=True)

    spatial = patches * spaces
    base_token = (me * (frames * spatial) + side * patches).astype(jnp.float32)
    row = lax.broadcasted_iota(jnp.int32, (rows, 1), 0).astype(jnp.float32)
    row_frame = count_floor(row, patches)
    token = base_token + row_frame * spatial + (row - row_frame * patches)
    lane = lax.broadcasted_iota(jnp.int32, (rows, LANES), 1)
    member = jnp.zeros((rows, LANES), jnp.float32)
    taken = jnp.zeros((rows, 1), jnp.float32)
    for group in range(owners):
        parity, rest = divmod(group, owners // 2)
        group_pair, group_side = divmod(rest, spaces)
        device = (group_pair * 2 + parity) * spaces + group_side
        hit = jnp.max(
            jnp.where(token == list_of(device), 1.0, 0.0), axis=1, keepdims=True
        )
        member += jnp.where(lane == group, hit, 0.0)
        taken += hit
    member += jnp.where(lane == owners, 1.0 - taken, 0.0)
    square_row = lax.broadcasted_iota(jnp.int32, (rows, rows), 0)
    square_lane = lax.broadcasted_iota(jnp.int32, (rows, rows), 1)
    before = small_dot(jnp.where(square_lane < square_row, 1.0, 0.0), member)
    group_base = jnp.where(lane < owners, lane * share, 0).astype(jnp.float32)
    place_of = jnp.sum(member * (before + group_base), axis=1, keepdims=True)
    counts = jnp.sum(member, axis=0, keepdims=True)
    group_row = lax.broadcasted_iota(jnp.int32, (LANES, rows), 0)
    group_lane = lax.broadcasted_iota(jnp.int32, (LANES, rows), 1)
    in_group = (group_lane >= group_row * share) & (group_lane < (group_row + 1) * share)
    held = small_dot(jnp.broadcast_to(counts, (8, LANES)), jnp.where(in_group, 1.0, 0.0))
    slot = lax.broadcasted_iota(jnp.int32, (8, rows), 1).astype(jnp.float32)
    free = jnp.where(slot - count_floor(slot, share) * share >= held, 1.0, 0.0)
    free_before = small_dot(free, jnp.where(square_row < square_lane, 1.0, 0.0))
    free_place = jnp.where(free > 0.5, free_before, -1.0)
    chosen = jnp.where(taken > 0.5, slot[0:1], free_place[0:1]) == place_of
    permuted = lax.dot_general(
        jnp.where(chosen, 1.0, 0.0).astype(jnp.bfloat16),
        x_ref[...],
        (((0,), (0,)), ((), ())),
        preferred_element_type=jnp.float32,
    ).astype(jnp.bfloat16)
    for half in range(2):
        for part in range(2):
            start = (half * 2 + part) * quarter
            own[part, half] = permuted[start : start + quarter]

    @pl.when(active)
    def _():
        for half in range(2):
            for part in range(2):
                start = (half * 2 + part) * quarter
                x_all[me, part, side, half] = permuted[start : start + quarter]

    pl.semaphore_wait(barrier, 7 + 2 * inner.astype(jnp.int32))

    def remote(source, target, send, receive, place):
        return pltpu.make_async_remote_copy(
            source, target, send, receive, device_id=place, device_id_type=MESH
        )

    def own_copy(kind, part, half):
        place = {
            0: {"clip": partner},
            1: {"space": other, "clip": core_clip(half)},
            2: {"tm": jnp.where(active, far, mate), "clip": core_clip(half)},
            3: {"tm": across, "clip": core_clip(half)},
        }[kind]
        return remote(
            own.at[part, half],
            x_all.at[me, part, side, half],
            own_sem.at[kind, part, half],
            recv.at[me, part, side, half],
            place,
        )

    near_part = (pair, 1 - pair)
    line_part = (jnp.where(active, 1 - pair, pair), jnp.where(active, pair, 1 - pair))
    across_part = (1 - pair, pair)
    send_across = idle & inner

    def line_sends(phase):
        for half in range(2):
            own_copy(2, line_part[phase], half).start()

        @pl.when(send_across)
        def _():
            for half in range(2):
                own_copy(3, across_part[phase], half).start()

    def near_sends(phase):
        @pl.when(active)
        def _():
            for half in range(2):
                own_copy(1, near_part[phase], half).start()
            for half in range(2):
                own_copy(0, near_part[phase], half).start()

    line_sends(0)

    @pl.when(idle & jnp.logical_not(inner))
    def _():
        for half in range(2):
            own_copy(2, line_part[1], half).start()

    near_sends(0)

    order = (
        me,
        mate,
        jnp.where(left, times // 2, times // 2 - 1),
        jnp.where(left, times - 1, 0),
    )

    def part_copy(place, phase, from_side, across_side):
        spot = (order[place], near_part[phase], from_side, core)
        return remote(
            x_all.at[spot], x_all.at[spot], part_sem.at[place, phase, across_side],
            recv.at[spot], {"clip": partner},
        )

    def side_copy(place, phase):
        spot = (order[place], near_part[phase], side, core)
        return remote(
            x_all.at[spot], x_all.at[spot], side_sem.at[place, phase],
            recv.at[spot], {"space": other},
        )

    def line_copy(phase):
        spot = (mate, near_part[phase], side, core)
        return remote(
            x_all.at[spot], x_all.at[spot], line_sem.at[phase], recv.at[spot], {"tm": far}
        )

    def landed(place, phase, from_side, half):
        spot = (order[place], near_part[phase], from_side, half)
        remote(
            x_all.at[spot], x_all.at[spot], part_sem.at[place, phase, 0],
            recv.at[spot], {"clip": partner},
        ).wait_recv()

    def arrive(place, phase):
        if place == 1 and phase == 1:

            @pl.when(jnp.logical_not(inner))
            def _():
                landed(place, phase, side, core)

        else:
            landed(place, phase, side, core)
        side_copy(place, phase).start()
        part_copy(place, phase, side, 0).start()
        if place == 1:
            if phase == 0:

                @pl.when(inner)
                def _():
                    landed(1, 1, side, core)
                    line_copy(1).start()

            else:

                @pl.when(inner)
                def _():
                    line_copy(0).start()

    def gather(place, phase):
        landed(place, phase, other, core)
        part_copy(place, phase, other, 1).start()
        if place == 0:

            @pl.when(idle)
            def _():
                landed(place, phase, side, 0)
                landed(place, phase, side, 1)

        else:
            landed(place, phase, side, 1 - core)
        landed(place, phase, other, 1 - core)

    def project(place, phase):
        gather(place, phase)
        normed[:rows, :] = norm_rows(
            x_all[order[place], near_part[phase]].reshape(rows, width),
            gain_ref[...],
            shift_ref[...],
        )
        start = (phase * times + place) * rows
        for part, weight, target in ((1, w_k, k_all), (2, w_v, v_all)):
            bias = b_qkv_ref[:, pl.ds(pl.multiple_of(part * width + column, LANES), span)]
            target[start : start + rows, :] = (
                jnp.dot(normed[:rows, :], weight[...], preferred_element_type=jnp.float32) + bias
            ).astype(jnp.bfloat16)

    score_scale = math.log2(math.e) / math.sqrt(head_width)
    half_heads = HEADS // 2
    groups = []
    head = 0
    while head < half_heads:
        base = min(head * head_width // LANES, span // LANES - 2) * LANES
        count = 1
        while (
            head + count < half_heads
            and (head + count + 1) * head_width + lane_skip <= base + WINDOW
        ):
            count += 1
        groups.append((base, range(head, head + count)))
        head += count
    skip = core * lane_skip

    def head_masks(height, base, heads):
        place = lax.broadcasted_iota(jnp.int32, (height, WINDOW), 1) + (base - skip)
        return [(place >= h * head_width) & (place < (h + 1) * head_width) for h in heads]

    def scores_of(row_slice, base, masks, key_start, key_end):
        window = queries[row_slice, base : base + WINDOW].astype(jnp.float32)
        stacked = jnp.concatenate(
            [jnp.where(mask, window, 0.0).astype(jnp.bfloat16) for mask in masks]
        )
        return lax.dot_general(
            stacked,
            k_all[key_start:key_end, base : base + WINDOW],
            (((1,), (1,)), ((), ())),
            preferred_element_type=jnp.float32,
        )

    split = times * rows
    all_keys = 2 * split

    def attend_first():
        sums[...] = jnp.zeros_like(sums)
        height = 2 * rows
        for base, heads in groups:
            masks = head_masks(height, base, heads)
            scores = scores_of(pl.ds(0, height), base, masks, 0, split)
            top = jnp.max(scores, axis=1, keepdims=True)
            weights = jnp.exp2((scores - top) * score_scale)
            summed = jnp.dot(
                weights.astype(jnp.bfloat16),
                v_all[0:split, base : base + WINDOW],
                preferred_element_type=jnp.float32,
            )
            counted = jnp.sum(weights, axis=1, keepdims=True)
            for place, h in enumerate(heads):
                part = slice(place * height, (place + 1) * height)
                high[h] = top[part]
                total[h] = counted[part]
                sums[:, base : base + WINDOW] += jnp.where(masks[place], summed[part], 0.0)

    def attend_rest(start):
        row_slice = pl.ds(start, rows)
        attended[row_slice, :] = jnp.zeros((rows, span), jnp.bfloat16)
        for base, heads in groups:
            masks = head_masks(rows, base, heads)
            scores = scores_of(row_slice, base, masks, split, all_keys)
            old = jnp.concatenate([high[h, row_slice, :] for h in heads])
            top = jnp.maximum(old, jnp.max(scores, axis=1, keepdims=True))
            weights = jnp.exp2((scores - top) * score_scale)
            factor = jnp.exp2((old - top) * score_scale)
            counted = jnp.concatenate([total[h, row_slice, :] for h in heads])
            counted = counted * factor + jnp.sum(weights, axis=1, keepdims=True)
            summed = jnp.dot(
                weights.astype(jnp.bfloat16),
                v_all[split:all_keys, base : base + WINDOW],
                preferred_element_type=jnp.float32,
            )
            carried = sums[row_slice, base : base + WINDOW]
            for place, h in enumerate(heads):
                part = slice(place * rows, (place + 1) * rows)
                result = (carried * factor[part] + summed[part]) / counted[part]
                kept = attended[row_slice, base : base + WINDOW].astype(jnp.float32)
                attended[row_slice, base : base + WINDOW] = jnp.where(
                    masks[place], result, kept
                ).astype(jnp.bfloat16)

    def make_queries():
        for parity in range(2):
            for block in range(times):
                for from_side in range(spaces):
                    piece = x_all[block, pair, from_side, parity].astype(jnp.float32)
                    start = parity * rows + (block * spaces + from_side) * share
                    rows_f32[start : start + share, :] = jnp.where(
                        side == 0, piece[:share], piece[share:]
                    )
        normed[...] = norm_rows(rows_f32[...], gain_ref[...], shift_ref[...])
        queries[...] = (
            jnp.dot(normed[...], w_q[...], preferred_element_type=jnp.float32)
            + b_qkv_ref[:, pl.ds(column, span)]
        ).astype(jnp.bfloat16)

    arrive(1, 0)
    line_sends_late = active | inner

    @pl.when(line_sends_late)
    def _():
        for half in range(2):
            own_copy(2, line_part[1], half).start()

    @pl.when(send_across)
    def _():
        for half in range(2):
            own_copy(3, across_part[1], half).start()

    near_sends(1)

    token_row = list_of(me * spaces + side)
    diagonal = square_row == square_lane

    def upright(values):
        return jnp.sum(jnp.where(diagonal, values, 0.0), axis=1, keepdims=True)

    def home_of(tokens):
        frame = count_floor(tokens, spatial)
        patch = tokens - frame * spatial
        block = count_floor(frame, frames)
        from_side = count_floor(patch, patches)
        inside = (frame - block * frames) * patches + patch - from_side * patches
        return block * spaces + from_side, inside

    token_column = upright(token_row)
    home_row, inside_row = home_of(token_row)
    home_column, inside_column = home_of(token_column)
    earlier = (
        (home_row == home_column) & (inside_row < inside_column) & (token_row >= 0)
    )
    rank = jnp.sum(jnp.where(earlier, 1.0, 0.0), axis=1, keepdims=True)
    wanted = home_column * share + rank
    found = (square_lane.astype(jnp.float32) == wanted) & (token_column >= 0)
    unpermute[...] = jnp.where(found, 1.0, 0.0).astype(jnp.bfloat16)

    for load in loads[:2]:
        load.wait()
    project(0, 0)
    arrive(2, 0)
    project(1, 0)
    arrive(3, 0)
    project(2, 0)
    arrive(1, 1)
    project(3, 0)
    loads[2].wait()
    make_queries()
    arrive(2, 1)
    project(0, 1)
    attend_first()
    arrive(3, 1)
    project(1, 1)
    project(2, 1)
    project(3, 1)
    loads[3].wait()

    def swap_copy(start):
        return remote(
            attended.at[pl.ds(start, rows)], attended_in, swap_sem.at[0], swap_sem.at[1],
            {"clip": partner},
        )

    back = remote(
        made_rows, back_rows, back_sem.at[0], back_sem.at[1],
        {"tm": mate, "clip": core_clip(1 - core)},
    )

    def finish(step, carried):
        owner = jnp.where(step == 0, 1 - active_core, active_core)
        start = pl.multiple_of(owner * rows, rows)
        attend_rest(start)

        @pl.when(owner != core)
        def _():
            swap_copy(start).start()

        @pl.when(owner == core)
        def _():
            swap_copy(start).wait_recv()
            mine = jnp.dot(
                attended[pl.ds(start, rows), :],
                w_out[pl.ds(pl.multiple_of(core * first_lane, LANES), span), :],
                preferred_element_type=jnp.float32,
            )
            theirs = jnp.dot(
                attended_in[...],
                w_out[pl.ds(pl.multiple_of((1 - core) * first_lane, LANES), span), :],
                preferred_element_type=jnp.float32,
            )
            hidden = (
                rows_f32[pl.ds(start, rows), :] + mine + theirs + b_out_ref[...]
            ).astype(jnp.bfloat16)
            made_rows[...] = layer_norm(
                hidden.astype(jnp.float32), final_gain_ref[...], final_shift_ref[...]
            ).astype(jnp.bfloat16)

            @pl.when(idle)
            def _():
                back.start()

        return carried

    lax.fori_loop(0, 2, finish, 0)

    def give(source):
        out_ref[0] = jnp.dot(
            unpermute[...], source[...], preferred_element_type=jnp.float32
        ).astype(jnp.bfloat16)

    @pl.when(active)
    def _():
        give(made_rows)

    @pl.when(idle)
    def _():
        back.wait_recv()
        give(back_rows)
        back.wait_send()

    swap_copy(pl.multiple_of((1 - core) * rows, rows)).wait_send()
    for phase in range(2):
        for half in range(2):
            own_copy(2, line_part[phase], half).wait_send()

            @pl.when(send_across)
            def _():
                own_copy(3, across_part[phase], half).wait_send()

            @pl.when(active)
            def _():
                own_copy(1, near_part[phase], half).wait_send()
                own_copy(0, near_part[phase], half).wait_send()

        for place in range(times):
            part_copy(place, phase, other, 1).wait_send()
            if place:
                part_copy(place, phase, side, 0).wait_send()
                side_copy(place, phase).wait_send()

        @pl.when(inner)
        def _():
            line_copy(phase).wait_send()


def fits_fused(times, spaces, clips, rows, width, owners, capacity):
    all_rows = times * spaces * rows
    held = 2 * (all_rows * width * 3 + width * width * 4 + 6 * rows * width)
    held += 4 * capacity * (width * 6 + all_rows * 6)
    share = capacity // owners
    return (
        spaces == 2
        and times == 4
        and clips % 2 == 0
        and held < VMEM_LIMIT
        and width % LANES == 0
        and HEADS % 2 == 0
        and width // HEADS <= LANES
        and owners == times * spaces
        and share * owners == capacity == rows
        and share % 8 == 0
        and rows % 64 == 0
    )


def fused_local(
    activations,
    attn_gain,
    attn_shift,
    w_qkv,
    b_qkv,
    w_out,
    b_out,
    final_gain,
    final_shift,
    mask_tokens,
    assignment,
):
    frames, patches, width = activations.shape
    rows = frames * patches
    times = lax.axis_size("tm")
    spaces = lax.axis_size("space")
    clips = lax.axis_size("clip")
    owners, capacity = mask_tokens.shape
    if not fits_fused(times, spaces, clips, rows, width, owners, capacity):
        return local(
            activations, attn_gain, attn_shift, w_qkv, b_qkv, w_out, b_out,
            final_gain, final_shift, mask_tokens, assignment,
        )
    half_width = width // 2
    span = width - half_width // LANES * LANES
    quarter = rows // 4
    keys = times * spaces * rows
    half_heads = HEADS // 2
    vmem = pl.BlockSpec(memory_space=pltpu.VMEM)
    hbm = pl.BlockSpec(memory_space=pl.ANY)
    smem = pl.BlockSpec(memory_space=pltpu.SMEM)
    bf16, f32 = jnp.bfloat16, jnp.float32
    dma = pltpu.SemaphoreType.DMA
    return pl.pallas_call(
        functools.partial(fused_kernel, times, spaces, frames, patches, width // HEADS),
        out_shape=jax.ShapeDtypeStruct((1, capacity, width), bf16),
        in_specs=[vmem, vmem, vmem, hbm, vmem, hbm, vmem, vmem, vmem, vmem, smem],
        out_specs=vmem,
        scratch_shapes=[
            pltpu.VMEM((2, 2, quarter, width), bf16),
            pltpu.VMEM((times, 2, spaces, 2, quarter, width), bf16),
            pltpu.VMEM((keys, span), bf16),
            pltpu.VMEM((keys, span), bf16),
            pltpu.VMEM((width, span), bf16),
            pltpu.VMEM((width, span), bf16),
            pltpu.VMEM((width, span), bf16),
            pltpu.VMEM((width, width), bf16),
            pltpu.VMEM((2 * rows, width), bf16),
            pltpu.VMEM((2 * rows, width), f32),
            pltpu.VMEM((2 * rows, span), bf16),
            pltpu.VMEM((2 * rows, span), f32),
            pltpu.VMEM((half_heads, 2 * rows, 1), f32),
            pltpu.VMEM((half_heads, 2 * rows, 1), f32),
            pltpu.VMEM((2 * rows, span), bf16),
            pltpu.VMEM((rows, span), bf16),
            pltpu.VMEM((rows, width), bf16),
            pltpu.VMEM((rows, width), bf16),
            pltpu.VMEM((rows, rows), bf16),
            pltpu.VMEM((1, 3 * width), f32),
            pltpu.VMEM((5, width), f32),
            dma((4,)),
            dma((4, 2, 2)),
            dma((times, 2, 2)),
            dma((times, 2)),
            dma((2,)),
            dma((times, 2, spaces, 2)),
            dma((2,)),
            dma((2,)),
        ],
        compiler_params=pltpu.CompilerParams(
            collective_id=0, has_side_effects=True, vmem_limit_bytes=VMEM_LIMIT
        ),
    )(
        activations.reshape(rows, width),
        attn_gain,
        attn_shift,
        w_qkv,
        b_qkv,
        w_out,
        b_out,
        final_gain,
        final_shift,
        mask_tokens,
        assignment,
    )


def solution(mesh):
    in_specs = (
        P(("clip", "tm"), "space", None),
        P(),
        P(),
        P(),
        P(),
        P(),
        P(),
        P(),
        P(),
        P("clip", None),
        P("clip"),
    )
    out_specs = P(("clip", "tm", "space"), None, None)
    return jax.shard_map(fused_local, mesh=mesh, in_specs=in_specs, out_specs=out_specs, check_vma=False)
```

```python
import functools
import math

import jax
import jax.numpy as jnp
from jax import lax
from jax.experimental import pallas as pl
from jax.experimental.pallas import tpu as pltpu
from jax.sharding import PartitionSpec as P

HEADS = 16


EPSILON = 1e-06
FLOOR_SCORE = -1e30


def layer_norm(values, ln_gain, ln_shift):
    centre = jnp.mean(values, axis=-1, keepdims=True)
    deviation = values - centre
    variance = jnp.mean(deviation * deviation, axis=-1, keepdims=True)
    return deviation * lax.rsqrt(variance + EPSILON) * ln_gain + ln_shift


def start_state(query_heads):
    query_count, head_count, head_width = query_heads.shape
    return (
        jnp.full((head_count, query_count), FLOOR_SCORE, jnp.float32),
        jnp.zeros((head_count, query_count), jnp.float32),
        jnp.zeros((head_count, query_count, head_width), jnp.float32),
    )


def finish_state(carried_state):
    running_max, running_total, running_sum = carried_state
    return jnp.transpose(running_sum / running_total[:, :, None], (1, 0, 2)).astype(jnp.bfloat16)


def make_attend(query_heads):
    query_count, head_count, head_width = query_heads.shape
    score_scale = 1.0 / math.sqrt(head_width)

    def one_block(carried_state, kv_block):
        running_max, running_total, running_sum = carried_state
        block_length = kv_block.shape[1]
        key_rows = kv_block[0].reshape(block_length, head_count, head_width)
        value_rows = kv_block[1].reshape(block_length, head_count, head_width)
        scores = (
            jnp.einsum("qhe,khe->hqk", query_heads, key_rows, preferred_element_type=jnp.float32)
            * score_scale
        )
        new_max = jnp.maximum(running_max, jnp.max(scores, axis=-1))
        factor = jnp.exp(running_max - new_max)
        weights = jnp.exp(scores - new_max[:, :, None])
        running_total = running_total * factor + jnp.sum(weights, axis=-1)
        running_sum = running_sum * factor[:, :, None] + jnp.einsum(
            "hqk,khe->hqe",
            weights.astype(jnp.bfloat16),
            value_rows,
            preferred_element_type=jnp.float32,
        )
        return (new_max, running_total, running_sum)

    def attend(carried_state, key_piece, first_row):
        length = key_piece.shape[1]
        block_rows = length
        while block_rows > 1024 and block_rows % 2 == 0:
            block_rows = block_rows // 2

        def advance(position, carried):
            kv_block = lax.dynamic_slice_in_dim(key_piece, position * block_rows, block_rows, 1)
            return one_block(carried, kv_block)

        return lax.fori_loop(0, length // block_rows, advance, carried_state)

    return attend


def local(
    activations,
    attn_gain,
    attn_shift,
    w_qkv,
    b_qkv,
    w_out,
    b_out,
    final_gain,
    final_shift,
    mask_tokens,
    assignment,
):
    frame_count, patch_count, model_width = activations.shape
    local_rows = frame_count * patch_count
    head_width = model_width // HEADS
    tokens_flat = activations.reshape(local_rows, model_width)
    normed_in = layer_norm(tokens_flat.astype(jnp.float32), attn_gain, attn_shift).astype(
        jnp.bfloat16
    )
    projected = (jnp.dot(normed_in, w_qkv, preferred_element_type=jnp.float32) + b_qkv).astype(
        jnp.bfloat16
    )
    query_rows = projected[:, :model_width]
    paired = jnp.stack(
        (projected[:, model_width : 2 * model_width], projected[:, 2 * model_width :])
    )
    groups = lax.axis_size("space")
    group_heads = HEADS // groups
    stacked = jnp.stack((query_rows, paired[0], paired[1])).reshape(
        3, local_rows, groups, group_heads, head_width
    )
    swapped = lax.all_to_all(stacked, "space", split_axis=2, concat_axis=1, tiled=True)
    gathered_rows = swapped.shape[1]
    kept_heads = swapped.shape[3]
    query_heads = swapped[0].reshape(gathered_rows, kept_heads, head_width)
    kv_rows = swapped[1:].reshape(2, gathered_rows, kept_heads * head_width)
    time_state = make_attend(query_heads)(
        start_state(query_heads), lax.all_gather(kv_rows, "tm", axis=1, tiled=True), jnp.int32(0)
    )
    head_output = finish_state(time_state).reshape(gathered_rows, 1, kept_heads, head_width)
    merged = lax.all_to_all(head_output, "space", split_axis=0, concat_axis=1, tiled=True)
    attended = merged.reshape(local_rows, model_width)
    hidden = (
        tokens_flat.astype(jnp.float32)
        + jnp.dot(attended, w_out, preferred_element_type=jnp.float32)
        + b_out
    ).astype(jnp.bfloat16)
    normed = layer_norm(hidden.astype(jnp.float32), final_gain, final_shift).astype(jnp.bfloat16)
    owners = mask_tokens.shape[0]
    capacity = mask_tokens.shape[1]
    per_source = capacity // owners
    spaces = lax.axis_size("space")
    spatial = patch_count * spaces
    own_index = lax.axis_index("tm") * spaces + lax.axis_index("space")
    owner_lists = jnp.take(mask_tokens, assignment, axis=0)
    listed = owner_lists >= 0
    clipped = jnp.maximum(owner_lists, 0)
    token_frame = clipped // spatial
    token_patch = clipped % spatial
    home_device = token_frame // frame_count * spaces + token_patch // patch_count
    local_row = token_frame % frame_count * patch_count + token_patch % patch_count
    mine = listed & (home_device == own_index)
    slot_index = jnp.cumsum(mine.astype(jnp.int32), axis=1) - 1
    wanted = mine[:, None, :] & (
        slot_index[:, None, :] == jnp.arange(per_source, dtype=jnp.int32)[None, :, None]
    )
    picks = jnp.sum(jnp.where(wanted, local_row[:, None, :], 0), axis=-1)
    present = jnp.any(wanted, axis=-1)
    own_home = lax.dynamic_index_in_dim(home_device, own_index, 0, keepdims=False)
    own_listed = lax.dynamic_index_in_dim(listed, own_index, 0, keepdims=False)
    entry_order = jnp.arange(capacity, dtype=jnp.int32)
    earlier = (
        (entry_order[:, None] < entry_order[None, :])
        & own_listed[:, None]
        & (own_home[:, None] == own_home[None, :])
    )
    entry_rank = jnp.sum(earlier.astype(jnp.int32), axis=0)
    where_from = jnp.where(own_listed, own_home * per_source + entry_rank, 0)
    outgoing = jnp.where(
        present[:, :, None], jnp.take(normed, picks, axis=0), jnp.zeros((), jnp.bfloat16)
    )
    arrived = lax.all_to_all(outgoing, ("tm", "space"), split_axis=0, concat_axis=0, tiled=True)
    row_table = arrived.reshape(owners * per_source, model_width)
    placed = jnp.take(row_table, where_from, axis=0)
    return jnp.where(own_listed[:, None], placed, jnp.zeros((), jnp.bfloat16))[None]


LANES = 128
WINDOW = 256
VMEM_LIMIT = 60 * 1024 * 1024
MESH = pl.DeviceIdType.MESH


def norm_rows(values, gain, shift):
    return layer_norm(values.astype(jnp.float32), gain, shift).astype(jnp.bfloat16)


def count_floor(values, size):
    return jnp.floor((values + 0.5) * (1.0 / size))


def small_dot(left, right):
    return jnp.dot(
        left.astype(jnp.bfloat16), right.astype(jnp.bfloat16), preferred_element_type=jnp.float32
    )


def fused_kernel(
    times,
    spaces,
    frames,
    patches,
    head_width,
    x_ref,
    gain_flat,
    shift_flat,
    w_qkv_ref,
    b_qkv_flat,
    w_out_ref,
    b_out_flat,
    final_gain_flat,
    final_shift_flat,
    lists_ref,
    assignment_ref,
    out_ref,
    own,
    x_all,
    k_all,
    v_all,
    w_q,
    w_k,
    w_v,
    w_out,
    normed,
    rows_f32,
    queries,
    sums,
    attended,
    attended_in,
    made_rows,
    back_rows,
    unpermute,
    b_qkv_ref,
    vectors,
    load_sem,
    own_sem,
    part_sem,
    side_sem,
    line_sem,
    recv,
    swap_sem,
    back_sem,
):
    me = lax.axis_index("tm")
    side = lax.axis_index("space")
    clip = lax.axis_index("clip")
    core = lax.rem(clip, 2)
    other = 1 - side
    partner = clip + 1 - 2 * core
    mate = me + 1 - 2 * lax.rem(me, 2)
    pair = lax.div(me, 2)
    far = lax.rem(me + 2, times)
    across = times - 1 - me
    active_core = lax.rem(me, 2)
    active = core == active_core
    idle = core != active_core
    inner = (me > 0) & (me < times - 1)
    left = me < times // 2
    rows, width = x_ref.shape
    quarter = rows // 4
    share = quarter // spaces
    owners, capacity = lists_ref.shape
    half_width = width // 2
    first_lane = half_width // LANES * LANES
    span = width - first_lane
    lane_skip = half_width - first_lane

    def core_clip(parity):
        return clip - core + parity

    column = pl.multiple_of(core * first_lane, LANES)
    loads = [
        pltpu.make_async_copy(
            w_qkv_ref.at[:, pl.ds(pl.multiple_of(part * width + column, LANES), span)],
            place,
            load_sem.at[part],
        )
        for part, place in ((1, w_k), (2, w_v), (0, w_q))
    ]
    loads.append(pltpu.make_async_copy(w_out_ref, w_out, load_sem.at[3]))
    for load in loads:
        load.start()

    barrier = pltpu.get_barrier_semaphore()

    def greet(**place):
        pl.semaphore_signal(barrier, inc=1, device_id=place, device_id_type=MESH)

    greet(clip=partner)
    for parity in range(2):
        greet(space=other, clip=core_clip(parity))
        greet(tm=mate, clip=core_clip(parity))
        greet(tm=far, clip=core_clip(parity))

        @pl.when(inner)
        def _():
            greet(tm=across, clip=core_clip(parity))

    b_qkv_ref[...] = b_qkv_flat[...].reshape(1, 3 * width)
    flats = (gain_flat, shift_flat, b_out_flat, final_gain_flat, final_shift_flat)
    for place, flat in enumerate(flats):
        vectors[place : place + 1, :] = flat[...].reshape(1, width)
    gain_ref, shift_ref, b_out_ref, final_gain_ref, final_shift_ref = (
        vectors.at[place : place + 1, :] for place in range(len(flats))
    )

    lists = lists_ref[...].astype(jnp.float32)
    list_places = lax.broadcasted_iota(jnp.int32, lists.shape, 0)

    def list_of(device):
        owner = assignment_ref[device]
        return jnp.sum(jnp.where(list_places == owner, lists, 0.0), axis=0, keepdims=True)

    spatial = patches * spaces
    base_token = (me * (frames * spatial) + side * patches).astype(jnp.float32)
    row = lax.broadcasted_iota(jnp.int32, (rows, 1), 0).astype(jnp.float32)
    row_frame = count_floor(row, patches)
    token = base_token + row_frame * spatial + (row - row_frame * patches)
    lane = lax.broadcasted_iota(jnp.int32, (rows, LANES), 1)
    member = jnp.zeros((rows, LANES), jnp.float32)
    taken = jnp.zeros((rows, 1), jnp.float32)
    for group in range(owners):
        parity, rest = divmod(group, owners // 2)
        group_pair, group_side = divmod(rest, spaces)
        device = (group_pair * 2 + parity) * spaces + group_side
        hit = jnp.max(
            jnp.where(token == list_of(device), 1.0, 0.0), axis=1, keepdims=True
        )
        member += jnp.where(lane == group, hit, 0.0)
        taken += hit
    member += jnp.where(lane == owners, 1.0 - taken, 0.0)
    square_row = lax.broadcasted_iota(jnp.int32, (rows, rows), 0)
    square_lane = lax.broadcasted_iota(jnp.int32, (rows, rows), 1)
    before = small_dot(jnp.where(square_lane < square_row, 1.0, 0.0), member)
    group_base = jnp.where(lane < owners, lane * share, 0).astype(jnp.float32)
    place_of = jnp.sum(member * (before + group_base), axis=1, keepdims=True)
    counts = jnp.sum(member, axis=0, keepdims=True)
    group_row = lax.broadcasted_iota(jnp.int32, (LANES, rows), 0)
    group_lane = lax.broadcasted_iota(jnp.int32, (LANES, rows), 1)
    in_group = (group_lane >= group_row * share) & (group_lane < (group_row + 1) * share)
    held = small_dot(jnp.broadcast_to(counts, (8, LANES)), jnp.where(in_group, 1.0, 0.0))
    slot = lax.broadcasted_iota(jnp.int32, (8, rows), 1).astype(jnp.float32)
    free = jnp.where(slot - count_floor(slot, share) * share >= held, 1.0, 0.0)
    free_before = small_dot(free, jnp.where(square_row < square_lane, 1.0, 0.0))
    free_place = jnp.where(free > 0.5, free_before, -1.0)
    chosen = jnp.where(taken > 0.5, slot[0:1], free_place[0:1]) == place_of
    permuted = lax.dot_general(
        jnp.where(chosen, 1.0, 0.0).astype(jnp.bfloat16),
        x_ref[...],
        (((0,), (0,)), ((), ())),
        preferred_element_type=jnp.float32,
    ).astype(jnp.bfloat16)
    for half in range(2):
        for part in range(2):
            start = (half * 2 + part) * quarter
            own[part, half] = permuted[start : start + quarter]

    @pl.when(active)
    def _():
        for half in range(2):
            for part in range(2):
                start = (half * 2 + part) * quarter
                x_all[me, part, side, half] = permuted[start : start + quarter]

    pl.semaphore_wait(barrier, 7 + 2 * inner.astype(jnp.int32))

    def remote(source, target, send, receive, place):
        return pltpu.make_async_remote_copy(
            source, target, send, receive, device_id=place, device_id_type=MESH
        )

    def own_copy(kind, part, half):
        place = {
            0: {"clip": partner},
            1: {"space": other, "clip": core_clip(half)},
            2: {"tm": jnp.where(active, far, mate), "clip": core_clip(half)},
            3: {"tm": across, "clip": core_clip(half)},
        }[kind]
        return remote(
            own.at[part, half],
            x_all.at[me, part, side, half],
            own_sem.at[kind, part, half],
            recv.at[me, part, side, half],
            place,
        )

    near_part = (pair, 1 - pair)
    line_part = (1 - pair, pair)
    send_across = idle & inner

    def line_sends(phase):
        for half in range(2):
            own_copy(2, line_part[phase], half).start()

        @pl.when(send_across)
        def _():
            for half in range(2):
                own_copy(3, line_part[phase], half).start()

    def near_sends(phase):
        @pl.when(active)
        def _():
            for half in range(2):
                own_copy(1, near_part[phase], half).start()
            for half in range(2):
                own_copy(0, near_part[phase], half).start()

    line_sends(0)
    near_sends(0)
    line_sends(1)
    near_sends(1)

    order = (
        me,
        mate,
        jnp.where(left, times // 2, times // 2 - 1),
        jnp.where(left, times - 1, 0),
    )

    def part_copy(place, phase, from_side, across_side):
        spot = (order[place], near_part[phase], from_side, core)
        return remote(
            x_all.at[spot], x_all.at[spot], part_sem.at[place, phase, across_side],
            recv.at[spot], {"clip": partner},
        )

    def side_copy(place, phase):
        spot = (order[place], near_part[phase], side, core)
        return remote(
            x_all.at[spot], x_all.at[spot], side_sem.at[place, phase],
            recv.at[spot], {"space": other},
        )

    def line_copy(phase):
        spot = (mate, near_part[phase], side, core)
        return remote(
            x_all.at[spot], x_all.at[spot], line_sem.at[phase], recv.at[spot], {"tm": far}
        )

    def landed(place, phase, from_side, half):
        spot = (order[place], near_part[phase], from_side, half)
        remote(
            x_all.at[spot], x_all.at[spot], part_sem.at[place, phase, 0],
            recv.at[spot], {"clip": partner},
        ).wait_recv()

    def arrive(place, phase):
        landed(place, phase, side, core)
        if place == 1:

            @pl.when(inner)
            def _():
                line_copy(phase).start()

        side_copy(place, phase).start()
        part_copy(place, phase, side, 0).start()

    def relay(place, phase):
        landed(place, phase, other, core)
        part_copy(place, phase, other, 1).start()

    def gather(place, phase):
        if place == 0:

            @pl.when(idle)
            def _():
                landed(place, phase, side, 0)
                landed(place, phase, side, 1)

        else:
            landed(place, phase, side, 1 - core)
        landed(place, phase, other, 1 - core)

    def project(place, phase):
        if (place, phase) != (3, 0):
            gather(place, phase)
        normed[:rows, :] = norm_rows(
            x_all[order[place], near_part[phase]].reshape(rows, width),
            gain_ref[...],
            shift_ref[...],
        )
        start = (phase * times + place) * rows
        for part, weight, target in ((1, w_k, k_all), (2, w_v, v_all)):
            bias = b_qkv_ref[:, pl.ds(pl.multiple_of(part * width + column, LANES), span)]
            target[start : start + rows, :] = (
                jnp.dot(normed[:rows, :], weight[...], preferred_element_type=jnp.float32) + bias
            ).astype(jnp.bfloat16)

    score_scale = math.log2(math.e) / math.sqrt(head_width)
    half_heads = HEADS // 2
    groups = []
    head = 0
    while head < half_heads:
        base = min(head * head_width // LANES, span // LANES - 2) * LANES
        count = 1
        while (
            head + count < half_heads
            and (head + count + 1) * head_width + lane_skip <= base + WINDOW
        ):
            count += 1
        groups.append((base, range(head, head + count)))
        head += count
    skip = core * lane_skip

    def head_masks(height, base, heads):
        place = lax.broadcasted_iota(jnp.int32, (height, WINDOW), 1) + (base - skip)
        return [(place >= h * head_width) & (place < (h + 1) * head_width) for h in heads]

    def scores_of(row_slice, base, masks, key_start, key_end):
        window = queries[row_slice, base : base + WINDOW].astype(jnp.float32)
        stacked = jnp.concatenate(
            [jnp.where(mask, window, 0.0).astype(jnp.bfloat16) for mask in masks]
        )
        return lax.dot_general(
            stacked,
            k_all[key_start:key_end, base : base + WINDOW],
            (((1,), (1,)), ((), ())),
            preferred_element_type=jnp.float32,
        )

    all_keys = 2 * times * rows

    def attend_all(start, height):
        row_slice = pl.ds(start, height)
        sums[row_slice, :] = jnp.zeros((height, span), jnp.float32)
        for base, heads in groups:
            masks = head_masks(height, base, heads)
            scores = scores_of(row_slice, base, masks, 0, all_keys)
            top = jnp.max(scores, axis=1, keepdims=True)
            weights = jnp.exp2((scores - top) * score_scale)
            counted = jnp.sum(weights, axis=1, keepdims=True)
            summed = jnp.dot(
                weights.astype(jnp.bfloat16),
                v_all[:, base : base + WINDOW],
                preferred_element_type=jnp.float32,
            ) / counted
            result = jnp.where(masks[0], summed[:height], 0.0)
            for place in range(1, len(heads)):
                result = jnp.where(
                    masks[place], summed[place * height : (place + 1) * height], result
                )
            sums[row_slice, base : base + WINDOW] += result
        attended[row_slice, :] = sums[row_slice, :].astype(jnp.bfloat16)

    def make_queries():
        for parity in range(2):
            for block in range(times):
                for from_side in range(spaces):
                    piece = x_all[block, pair, from_side, parity].astype(jnp.float32)
                    start = parity * rows + (block * spaces + from_side) * share
                    rows_f32[start : start + share, :] = jnp.where(
                        side == 0, piece[:share], piece[share:]
                    )
        normed[...] = norm_rows(rows_f32[...], gain_ref[...], shift_ref[...])
        queries[...] = (
            jnp.dot(normed[...], w_q[...], preferred_element_type=jnp.float32)
            + b_qkv_ref[:, pl.ds(column, span)]
        ).astype(jnp.bfloat16)

    arrive(1, 1)
    arrive(1, 0)

    token_row = list_of(me * spaces + side)
    diagonal = square_row == square_lane

    def upright(values):
        return jnp.sum(jnp.where(diagonal, values, 0.0), axis=1, keepdims=True)

    def home_of(tokens):
        frame = count_floor(tokens, spatial)
        patch = tokens - frame * spatial
        block = count_floor(frame, frames)
        from_side = count_floor(patch, patches)
        inside = (frame - block * frames) * patches + patch - from_side * patches
        return block * spaces + from_side, inside

    token_column = upright(token_row)
    home_row, inside_row = home_of(token_row)
    home_column, inside_column = home_of(token_column)
    earlier = (
        (home_row == home_column) & (inside_row < inside_column) & (token_row >= 0)
    )
    rank = jnp.sum(jnp.where(earlier, 1.0, 0.0), axis=1, keepdims=True)
    wanted = home_column * share + rank
    found = (square_lane.astype(jnp.float32) == wanted) & (token_column >= 0)
    unpermute[...] = jnp.where(found, 1.0, 0.0).astype(jnp.bfloat16)

    for load in loads[:2]:
        load.wait()
    relay(0, 0)
    project(0, 0)
    relay(0, 1)
    project(0, 1)
    relay(1, 1)
    arrive(2, 0)
    project(1, 1)
    relay(1, 0)
    project(1, 0)
    arrive(2, 1)
    relay(2, 0)
    project(2, 0)
    arrive(3, 0)
    relay(2, 1)
    project(2, 1)
    relay(3, 0)
    arrive(3, 1)
    loads[2].wait()
    gather(3, 0)
    make_queries()
    relay(3, 1)
    project(3, 0)
    project(3, 1)
    loads[3].wait()

    def swap_copy(start):
        return remote(
            attended.at[pl.ds(start, rows)], attended_in, swap_sem.at[0], swap_sem.at[1],
            {"clip": partner},
        )

    chunk = rows // 2

    def back_copy(step):
        piece = pl.ds(pl.multiple_of(step * chunk, chunk), chunk)
        return remote(
            made_rows.at[piece], back_rows.at[piece], back_sem.at[0, step], back_sem.at[1, step],
            {"tm": mate, "clip": core_clip(1 - core)},
        )

    def finish(step, carried):
        owner = jnp.where(step == 0, 1 - active_core, active_core)
        start = pl.multiple_of(owner * rows, rows)
        attend_all(start, rows)

        @pl.when(owner != core)
        def _():
            swap_copy(start).start()

        @pl.when(owner == core)
        def _():
            def close(step, carried):
                inside = pl.multiple_of(step * chunk, chunk)
                piece = pl.ds(pl.multiple_of(start + inside, chunk), chunk)
                mine = jnp.dot(
                    attended[piece, :],
                    w_out[pl.ds(pl.multiple_of(core * first_lane, LANES), span), :],
                    preferred_element_type=jnp.float32,
                )

                @pl.when(step == 0)
                def _():
                    swap_copy(start).wait_recv()

                theirs = jnp.dot(
                    attended_in[pl.ds(inside, chunk), :],
                    w_out[pl.ds(pl.multiple_of((1 - core) * first_lane, LANES), span), :],
                    preferred_element_type=jnp.float32,
                )
                hidden = (
                    rows_f32[piece, :] + mine + theirs + b_out_ref[...]
                ).astype(jnp.bfloat16)
                made_rows[pl.ds(inside, chunk), :] = layer_norm(
                    hidden.astype(jnp.float32), final_gain_ref[...], final_shift_ref[...]
                ).astype(jnp.bfloat16)

                @pl.when(idle)
                def _():
                    back_copy(step).start()

                return carried

            lax.fori_loop(0, 2, close, 0)

        return carried

    lax.fori_loop(0, 2, finish, 0)

    def give(source):
        out_ref[0] = jnp.dot(
            unpermute[...], source[...], preferred_element_type=jnp.float32
        ).astype(jnp.bfloat16)

    @pl.when(active)
    def _():
        give(made_rows)

    @pl.when(idle)
    def _():
        for step in range(2):
            back_copy(step).wait_recv()
        give(back_rows)
        for step in range(2):
            back_copy(step).wait_send()

    swap_copy(pl.multiple_of((1 - core) * rows, rows)).wait_send()
    for phase in range(2):
        for half in range(2):
            own_copy(2, line_part[phase], half).wait_send()

            @pl.when(send_across)
            def _():
                own_copy(3, line_part[phase], half).wait_send()

            @pl.when(active)
            def _():
                own_copy(1, near_part[phase], half).wait_send()
                own_copy(0, near_part[phase], half).wait_send()

        for place in range(times):
            part_copy(place, phase, other, 1).wait_send()
            if place:
                part_copy(place, phase, side, 0).wait_send()
                side_copy(place, phase).wait_send()

        @pl.when(inner)
        def _():
            line_copy(phase).wait_send()


def fits_fused(times, spaces, clips, rows, width, owners, capacity):
    all_rows = times * spaces * rows
    held = 2 * (all_rows * width * 3 + width * width * 4 + 6 * rows * width)
    held += 4 * capacity * (width * 6 + all_rows * 6)
    share = capacity // owners
    return (
        spaces == 2
        and times == 4
        and clips % 2 == 0
        and held < VMEM_LIMIT
        and width % LANES == 0
        and HEADS % 2 == 0
        and width // HEADS <= LANES
        and owners == times * spaces
        and share * owners == capacity == rows
        and share % 8 == 0
        and rows % 64 == 0
    )


def fused_local(
    activations,
    attn_gain,
    attn_shift,
    w_qkv,
    b_qkv,
    w_out,
    b_out,
    final_gain,
    final_shift,
    mask_tokens,
    assignment,
):
    frames, patches, width = activations.shape
    rows = frames * patches
    times = lax.axis_size("tm")
    spaces = lax.axis_size("space")
    clips = lax.axis_size("clip")
    owners, capacity = mask_tokens.shape
    if not fits_fused(times, spaces, clips, rows, width, owners, capacity):
        return local(
            activations, attn_gain, attn_shift, w_qkv, b_qkv, w_out, b_out,
            final_gain, final_shift, mask_tokens, assignment,
        )
    half_width = width // 2
    span = width - half_width // LANES * LANES
    quarter = rows // 4
    keys = times * spaces * rows
    vmem = pl.BlockSpec(memory_space=pltpu.VMEM)
    hbm = pl.BlockSpec(memory_space=pl.ANY)
    smem = pl.BlockSpec(memory_space=pltpu.SMEM)
    bf16, f32 = jnp.bfloat16, jnp.float32
    dma = pltpu.SemaphoreType.DMA
    return pl.pallas_call(
        functools.partial(fused_kernel, times, spaces, frames, patches, width // HEADS),
        out_shape=jax.ShapeDtypeStruct((1, capacity, width), bf16),
        in_specs=[vmem, vmem, vmem, hbm, vmem, hbm, vmem, vmem, vmem, vmem, smem],
        out_specs=vmem,
        scratch_shapes=[
            pltpu.VMEM((2, 2, quarter, width), bf16),
            pltpu.VMEM((times, 2, spaces, 2, quarter, width), bf16),
            pltpu.VMEM((keys, span), bf16),
            pltpu.VMEM((keys, span), bf16),
            pltpu.VMEM((width, span), bf16),
            pltpu.VMEM((width, span), bf16),
            pltpu.VMEM((width, span), bf16),
            pltpu.VMEM((width, width), bf16),
            pltpu.VMEM((2 * rows, width), bf16),
            pltpu.VMEM((2 * rows, width), f32),
            pltpu.VMEM((2 * rows, span), bf16),
            pltpu.VMEM((2 * rows, span), f32),
            pltpu.VMEM((2 * rows, span), bf16),
            pltpu.VMEM((rows, span), bf16),
            pltpu.VMEM((rows, width), bf16),
            pltpu.VMEM((rows, width), bf16),
            pltpu.VMEM((rows, rows), bf16),
            pltpu.VMEM((1, 3 * width), f32),
            pltpu.VMEM((5, width), f32),
            dma((4,)),
            dma((4, 2, 2)),
            dma((times, 2, 2)),
            dma((times, 2)),
            dma((2,)),
            dma((times, 2, spaces, 2)),
            dma((2,)),
            dma((2, 2)),
        ],
        compiler_params=pltpu.CompilerParams(
            collective_id=0, has_side_effects=True, vmem_limit_bytes=VMEM_LIMIT
        ),
    )(
        activations.reshape(rows, width),
        attn_gain,
        attn_shift,
        w_qkv,
        b_qkv,
        w_out,
        b_out,
        final_gain,
        final_shift,
        mask_tokens,
        assignment,
    )


def solution(mesh):
    in_specs = (
        P(("clip", "tm"), "space", None),
        P(),
        P(),
        P(),
        P(),
        P(),
        P(),
        P(),
        P(),
        P("clip", None),
        P("clip"),
    )
    out_specs = P(("clip", "tm", "space"), None, None)
    return jax.shard_map(fused_local, mesh=mesh, in_specs=in_specs, out_specs=out_specs, check_vma=False)
```

```python
import functools
import math

import jax
import jax.numpy as jnp
from jax import lax
from jax.experimental import pallas as pl
from jax.experimental.pallas import tpu as pltpu
from jax.sharding import PartitionSpec as P

HEADS = 16


EPSILON = 1e-06
FLOOR_SCORE = -1e30


def layer_norm(values, ln_gain, ln_shift):
    centre = jnp.mean(values, axis=-1, keepdims=True)
    deviation = values - centre
    variance = jnp.mean(deviation * deviation, axis=-1, keepdims=True)
    return deviation * lax.rsqrt(variance + EPSILON) * ln_gain + ln_shift


def start_state(query_heads):
    query_count, head_count, head_width = query_heads.shape
    return (
        jnp.full((head_count, query_count), FLOOR_SCORE, jnp.float32),
        jnp.zeros((head_count, query_count), jnp.float32),
        jnp.zeros((head_count, query_count, head_width), jnp.float32),
    )


def finish_state(carried_state):
    running_max, running_total, running_sum = carried_state
    return jnp.transpose(running_sum / running_total[:, :, None], (1, 0, 2)).astype(jnp.bfloat16)


def make_attend(query_heads):
    query_count, head_count, head_width = query_heads.shape
    score_scale = 1.0 / math.sqrt(head_width)

    def one_block(carried_state, kv_block):
        running_max, running_total, running_sum = carried_state
        block_length = kv_block.shape[1]
        key_rows = kv_block[0].reshape(block_length, head_count, head_width)
        value_rows = kv_block[1].reshape(block_length, head_count, head_width)
        scores = (
            jnp.einsum("qhe,khe->hqk", query_heads, key_rows, preferred_element_type=jnp.float32)
            * score_scale
        )
        new_max = jnp.maximum(running_max, jnp.max(scores, axis=-1))
        factor = jnp.exp(running_max - new_max)
        weights = jnp.exp(scores - new_max[:, :, None])
        running_total = running_total * factor + jnp.sum(weights, axis=-1)
        running_sum = running_sum * factor[:, :, None] + jnp.einsum(
            "hqk,khe->hqe",
            weights.astype(jnp.bfloat16),
            value_rows,
            preferred_element_type=jnp.float32,
        )
        return (new_max, running_total, running_sum)

    def attend(carried_state, key_piece, first_row):
        length = key_piece.shape[1]
        block_rows = length
        while block_rows > 1024 and block_rows % 2 == 0:
            block_rows = block_rows // 2

        def advance(position, carried):
            kv_block = lax.dynamic_slice_in_dim(key_piece, position * block_rows, block_rows, 1)
            return one_block(carried, kv_block)

        return lax.fori_loop(0, length // block_rows, advance, carried_state)

    return attend


def local(
    activations,
    attn_gain,
    attn_shift,
    w_qkv,
    b_qkv,
    w_out,
    b_out,
    final_gain,
    final_shift,
    mask_tokens,
    assignment,
):
    frame_count, patch_count, model_width = activations.shape
    local_rows = frame_count * patch_count
    head_width = model_width // HEADS
    tokens_flat = activations.reshape(local_rows, model_width)
    normed_in = layer_norm(tokens_flat.astype(jnp.float32), attn_gain, attn_shift).astype(
        jnp.bfloat16
    )
    projected = (jnp.dot(normed_in, w_qkv, preferred_element_type=jnp.float32) + b_qkv).astype(
        jnp.bfloat16
    )
    query_rows = projected[:, :model_width]
    paired = jnp.stack(
        (projected[:, model_width : 2 * model_width], projected[:, 2 * model_width :])
    )
    groups = lax.axis_size("space")
    group_heads = HEADS // groups
    stacked = jnp.stack((query_rows, paired[0], paired[1])).reshape(
        3, local_rows, groups, group_heads, head_width
    )
    swapped = lax.all_to_all(stacked, "space", split_axis=2, concat_axis=1, tiled=True)
    gathered_rows = swapped.shape[1]
    kept_heads = swapped.shape[3]
    query_heads = swapped[0].reshape(gathered_rows, kept_heads, head_width)
    kv_rows = swapped[1:].reshape(2, gathered_rows, kept_heads * head_width)
    time_state = make_attend(query_heads)(
        start_state(query_heads), lax.all_gather(kv_rows, "tm", axis=1, tiled=True), jnp.int32(0)
    )
    head_output = finish_state(time_state).reshape(gathered_rows, 1, kept_heads, head_width)
    merged = lax.all_to_all(head_output, "space", split_axis=0, concat_axis=1, tiled=True)
    attended = merged.reshape(local_rows, model_width)
    hidden = (
        tokens_flat.astype(jnp.float32)
        + jnp.dot(attended, w_out, preferred_element_type=jnp.float32)
        + b_out
    ).astype(jnp.bfloat16)
    normed = layer_norm(hidden.astype(jnp.float32), final_gain, final_shift).astype(jnp.bfloat16)
    owners = mask_tokens.shape[0]
    capacity = mask_tokens.shape[1]
    per_source = capacity // owners
    spaces = lax.axis_size("space")
    spatial = patch_count * spaces
    own_index = lax.axis_index("tm") * spaces + lax.axis_index("space")
    owner_lists = jnp.take(mask_tokens, assignment, axis=0)
    listed = owner_lists >= 0
    clipped = jnp.maximum(owner_lists, 0)
    token_frame = clipped // spatial
    token_patch = clipped % spatial
    home_device = token_frame // frame_count * spaces + token_patch // patch_count
    local_row = token_frame % frame_count * patch_count + token_patch % patch_count
    mine = listed & (home_device == own_index)
    slot_index = jnp.cumsum(mine.astype(jnp.int32), axis=1) - 1
    wanted = mine[:, None, :] & (
        slot_index[:, None, :] == jnp.arange(per_source, dtype=jnp.int32)[None, :, None]
    )
    picks = jnp.sum(jnp.where(wanted, local_row[:, None, :], 0), axis=-1)
    present = jnp.any(wanted, axis=-1)
    own_home = lax.dynamic_index_in_dim(home_device, own_index, 0, keepdims=False)
    own_listed = lax.dynamic_index_in_dim(listed, own_index, 0, keepdims=False)
    entry_order = jnp.arange(capacity, dtype=jnp.int32)
    earlier = (
        (entry_order[:, None] < entry_order[None, :])
        & own_listed[:, None]
        & (own_home[:, None] == own_home[None, :])
    )
    entry_rank = jnp.sum(earlier.astype(jnp.int32), axis=0)
    where_from = jnp.where(own_listed, own_home * per_source + entry_rank, 0)
    outgoing = jnp.where(
        present[:, :, None], jnp.take(normed, picks, axis=0), jnp.zeros((), jnp.bfloat16)
    )
    arrived = lax.all_to_all(outgoing, ("tm", "space"), split_axis=0, concat_axis=0, tiled=True)
    row_table = arrived.reshape(owners * per_source, model_width)
    placed = jnp.take(row_table, where_from, axis=0)
    return jnp.where(own_listed[:, None], placed, jnp.zeros((), jnp.bfloat16))[None]


LANES = 128
WINDOW = 256
VMEM_LIMIT = 60 * 1024 * 1024
MESH = pl.DeviceIdType.MESH


def norm_rows(values, gain, shift):
    return layer_norm(values.astype(jnp.float32), gain, shift).astype(jnp.bfloat16)


def count_floor(values, size):
    return jnp.floor((values + 0.5) * (1.0 / size))


def small_dot(left, right):
    return jnp.dot(
        left.astype(jnp.bfloat16), right.astype(jnp.bfloat16), preferred_element_type=jnp.float32
    )


def fused_kernel(
    times,
    spaces,
    frames,
    patches,
    head_width,
    x_ref,
    gain_flat,
    shift_flat,
    w_qkv_ref,
    b_qkv_flat,
    w_out_ref,
    b_out_flat,
    final_gain_flat,
    final_shift_flat,
    lists_ref,
    assignment_ref,
    out_ref,
    own,
    x_all,
    k_all,
    v_all,
    w_q,
    w_k,
    w_v,
    w_out,
    normed,
    rows_f32,
    queries,
    sums,
    attended,
    attended_in,
    made_rows,
    back_rows,
    unpermute,
    b_qkv_ref,
    vectors,
    load_sem,
    own_sem,
    part_sem,
    side_sem,
    line_sem,
    recv,
    swap_sem,
    back_sem,
):
    me = lax.axis_index("tm")
    side = lax.axis_index("space")
    clip = lax.axis_index("clip")
    core = lax.rem(clip, 2)
    other = 1 - side
    partner = clip + 1 - 2 * core
    mate = me + 1 - 2 * lax.rem(me, 2)
    pair = lax.div(me, 2)
    far = lax.rem(me + 2, times)
    across = times - 1 - me
    active_core = lax.rem(me, 2)
    active = core == active_core
    idle = core != active_core
    inner = (me > 0) & (me < times - 1)
    left = me < times // 2
    rows, width = x_ref.shape
    quarter = rows // 4
    share = quarter // spaces
    owners, capacity = lists_ref.shape
    half_width = width // 2
    first_lane = half_width // LANES * LANES
    span = width - first_lane
    lane_skip = half_width - first_lane

    def core_clip(parity):
        return clip - core + parity

    column = pl.multiple_of(core * first_lane, LANES)
    loads = [
        pltpu.make_async_copy(
            w_qkv_ref.at[:, pl.ds(pl.multiple_of(part * width + column, LANES), span)],
            place,
            load_sem.at[part],
        )
        for part, place in ((1, w_k), (2, w_v), (0, w_q))
    ]
    loads.append(pltpu.make_async_copy(w_out_ref, w_out, load_sem.at[3]))

    barrier = pltpu.get_barrier_semaphore()

    def greet(**place):
        pl.semaphore_signal(barrier, inc=1, device_id=place, device_id_type=MESH)

    greet(clip=partner)
    for parity in range(2):
        greet(space=other, clip=core_clip(parity))
        greet(tm=mate, clip=core_clip(parity))
        greet(tm=far, clip=core_clip(parity))

        @pl.when(inner)
        def _():
            greet(tm=across, clip=core_clip(parity))

    b_qkv_ref[...] = b_qkv_flat[...].reshape(1, 3 * width)
    flats = (gain_flat, shift_flat, b_out_flat, final_gain_flat, final_shift_flat)
    for place, flat in enumerate(flats):
        vectors[place : place + 1, :] = flat[...].reshape(1, width)
    gain_ref, shift_ref, b_out_ref, final_gain_ref, final_shift_ref = (
        vectors.at[place : place + 1, :] for place in range(len(flats))
    )

    lists = lists_ref[...].astype(jnp.float32)
    list_places = lax.broadcasted_iota(jnp.int32, lists.shape, 0)

    def list_of(device):
        owner = assignment_ref[device]
        return jnp.sum(jnp.where(list_places == owner, lists, 0.0), axis=0, keepdims=True)

    spatial = patches * spaces
    base_token = (me * (frames * spatial) + side * patches).astype(jnp.float32)
    row = lax.broadcasted_iota(jnp.int32, (rows, 1), 0).astype(jnp.float32)
    row_frame = count_floor(row, patches)
    token = base_token + row_frame * spatial + (row - row_frame * patches)
    lane = lax.broadcasted_iota(jnp.int32, (rows, LANES), 1)
    member = jnp.zeros((rows, LANES), jnp.float32)
    taken = jnp.zeros((rows, 1), jnp.float32)
    for group in range(owners):
        parity, rest = divmod(group, owners // 2)
        group_pair, group_side = divmod(rest, spaces)
        device = (group_pair * 2 + parity) * spaces + group_side
        hit = jnp.max(
            jnp.where(token == list_of(device), 1.0, 0.0), axis=1, keepdims=True
        )
        member += jnp.where(lane == group, hit, 0.0)
        taken += hit
    member += jnp.where(lane == owners, 1.0 - taken, 0.0)
    square_row = lax.broadcasted_iota(jnp.int32, (rows, rows), 0)
    square_lane = lax.broadcasted_iota(jnp.int32, (rows, rows), 1)
    before = small_dot(jnp.where(square_lane < square_row, 1.0, 0.0), member)
    group_base = jnp.where(lane < owners, lane * share, 0).astype(jnp.float32)
    place_of = jnp.sum(member * (before + group_base), axis=1, keepdims=True)
    counts = jnp.sum(member, axis=0, keepdims=True)
    group_row = lax.broadcasted_iota(jnp.int32, (LANES, rows), 0)
    group_lane = lax.broadcasted_iota(jnp.int32, (LANES, rows), 1)
    in_group = (group_lane >= group_row * share) & (group_lane < (group_row + 1) * share)
    held = small_dot(jnp.broadcast_to(counts, (8, LANES)), jnp.where(in_group, 1.0, 0.0))
    slot = lax.broadcasted_iota(jnp.int32, (8, rows), 1).astype(jnp.float32)
    free = jnp.where(slot - count_floor(slot, share) * share >= held, 1.0, 0.0)
    free_before = small_dot(free, jnp.where(square_row < square_lane, 1.0, 0.0))
    free_place = jnp.where(free > 0.5, free_before, -1.0)
    chosen = jnp.where(taken > 0.5, slot[0:1], free_place[0:1]) == place_of
    permuted = lax.dot_general(
        jnp.where(chosen, 1.0, 0.0).astype(jnp.bfloat16),
        x_ref[...],
        (((0,), (0,)), ((), ())),
        preferred_element_type=jnp.float32,
    ).astype(jnp.bfloat16)
    for half in range(2):
        for part in range(2):
            start = (half * 2 + part) * quarter
            own[part, half] = permuted[start : start + quarter]

    @pl.when(active)
    def _():
        for half in range(2):
            for part in range(2):
                start = (half * 2 + part) * quarter
                x_all[me, part, side, half] = permuted[start : start + quarter]

    pl.semaphore_wait(barrier, 7 + 2 * inner.astype(jnp.int32))

    def remote(source, target, send, receive, place):
        return pltpu.make_async_remote_copy(
            source, target, send, receive, device_id=place, device_id_type=MESH
        )

    def own_copy(kind, part, half):
        place = {
            0: {"clip": partner},
            1: {"space": other, "clip": core_clip(half)},
            2: {"tm": jnp.where(active, far, mate), "clip": core_clip(half)},
            3: {"tm": across, "clip": core_clip(half)},
        }[kind]
        return remote(
            own.at[part, half],
            x_all.at[me, part, side, half],
            own_sem.at[kind, part, half],
            recv.at[me, part, side, half],
            place,
        )

    near_part = (pair, 1 - pair)
    line_part = (1 - pair, pair)
    send_across = idle & inner

    def line_sends(phase):
        for half in range(2):
            own_copy(2, line_part[phase], half).start()

        @pl.when(send_across)
        def _():
            for half in range(2):
                own_copy(3, line_part[phase], half).start()

    def near_sends(phase):
        @pl.when(active)
        def _():
            for half in range(2):
                own_copy(1, near_part[phase], half).start()
            for half in range(2):
                own_copy(0, near_part[phase], half).start()

    near_sends(0)
    line_sends(0)
    near_sends(1)
    line_sends(1)
    for load in loads:
        load.start()

    order = (
        me,
        mate,
        jnp.where(left, times // 2, times // 2 - 1),
        jnp.where(left, times - 1, 0),
    )

    def part_copy(place, phase, from_side, across_side):
        spot = (order[place], near_part[phase], from_side, core)
        return remote(
            x_all.at[spot], x_all.at[spot], part_sem.at[place, phase, across_side],
            recv.at[spot], {"clip": partner},
        )

    def side_copy(place, phase):
        spot = (order[place], near_part[phase], side, core)
        return remote(
            x_all.at[spot], x_all.at[spot], side_sem.at[place, phase],
            recv.at[spot], {"space": other},
        )

    def line_copy(phase):
        spot = (mate, near_part[phase], side, core)
        return remote(
            x_all.at[spot], x_all.at[spot], line_sem.at[phase], recv.at[spot], {"tm": far}
        )

    def landed(place, phase, from_side, half):
        spot = (order[place], near_part[phase], from_side, half)
        remote(
            x_all.at[spot], x_all.at[spot], part_sem.at[place, phase, 0],
            recv.at[spot], {"clip": partner},
        ).wait_recv()

    def arrive(place, phase):
        landed(place, phase, side, core)
        if place == 1:

            @pl.when(inner)
            def _():
                line_copy(phase).start()

        side_copy(place, phase).start()
        part_copy(place, phase, side, 0).start()

    def relay(place, phase):
        landed(place, phase, other, core)
        part_copy(place, phase, other, 1).start()

    def gather(place, phase):
        if place == 0:

            @pl.when(idle)
            def _():
                landed(place, phase, side, 0)
                landed(place, phase, side, 1)

        else:
            landed(place, phase, side, 1 - core)
        landed(place, phase, other, 1 - core)

    def project(place, phase):
        if (place, phase) != (3, 0):
            gather(place, phase)
        normed[:rows, :] = norm_rows(
            x_all[order[place], near_part[phase]].reshape(rows, width),
            gain_ref[...],
            shift_ref[...],
        )
        start = (phase * times + place) * rows
        for part, weight, target in ((1, w_k, k_all), (2, w_v, v_all)):
            bias = b_qkv_ref[:, pl.ds(pl.multiple_of(part * width + column, LANES), span)]
            target[start : start + rows, :] = (
                jnp.dot(normed[:rows, :], weight[...], preferred_element_type=jnp.float32) + bias
            ).astype(jnp.bfloat16)

    score_scale = math.log2(math.e) / math.sqrt(head_width)
    half_heads = HEADS // 2
    groups = []
    head = 0
    while head < half_heads:
        base = min(head * head_width // LANES, span // LANES - 2) * LANES
        count = 1
        while (
            head + count < half_heads
            and (head + count + 1) * head_width + lane_skip <= base + WINDOW
        ):
            count += 1
        groups.append((base, range(head, head + count)))
        head += count
    skip = core * lane_skip

    def head_masks(height, base, heads):
        place = lax.broadcasted_iota(jnp.int32, (height, WINDOW), 1) + (base - skip)
        return [(place >= h * head_width) & (place < (h + 1) * head_width) for h in heads]

    def scores_of(row_slice, base, masks, key_start, key_end):
        window = queries[row_slice, base : base + WINDOW].astype(jnp.float32)
        stacked = jnp.concatenate(
            [jnp.where(mask, window, 0.0).astype(jnp.bfloat16) for mask in masks]
        )
        return lax.dot_general(
            stacked,
            k_all[key_start:key_end, base : base + WINDOW],
            (((1,), (1,)), ((), ())),
            preferred_element_type=jnp.float32,
        )

    all_keys = 2 * times * rows

    def attend_all(start, height):
        row_slice = pl.ds(start, height)
        sums[row_slice, :] = jnp.zeros((height, span), jnp.float32)
        for base, heads in groups:
            masks = head_masks(height, base, heads)
            scores = scores_of(row_slice, base, masks, 0, all_keys)
            top = jnp.max(scores, axis=1, keepdims=True)
            weights = jnp.exp2((scores - top) * score_scale)
            inverse = 1.0 / jnp.sum(weights, axis=1, keepdims=True)
            summed = jnp.dot(
                weights.astype(jnp.bfloat16),
                v_all[:, base : base + WINDOW],
                preferred_element_type=jnp.float32,
            ) * inverse
            result = jnp.where(masks[0], summed[:height], 0.0)
            for place in range(1, len(heads)):
                result = jnp.where(
                    masks[place], summed[place * height : (place + 1) * height], result
                )
            sums[row_slice, base : base + WINDOW] += result
        attended[row_slice, :] = sums[row_slice, :].astype(jnp.bfloat16)

    def make_queries():
        for parity in range(2):
            for block in range(times):
                for from_side in range(spaces):
                    piece = x_all[block, pair, from_side, parity].astype(jnp.float32)
                    start = parity * rows + (block * spaces + from_side) * share
                    rows_f32[start : start + share, :] = jnp.where(
                        side == 0, piece[:share], piece[share:]
                    )
        normed[...] = norm_rows(rows_f32[...], gain_ref[...], shift_ref[...])
        queries[...] = (
            jnp.dot(normed[...], w_q[...], preferred_element_type=jnp.float32)
            + b_qkv_ref[:, pl.ds(column, span)]
        ).astype(jnp.bfloat16)

    arrive(1, 1)
    arrive(1, 0)

    token_row = list_of(me * spaces + side)
    diagonal = square_row == square_lane

    def upright(values):
        return jnp.sum(jnp.where(diagonal, values, 0.0), axis=1, keepdims=True)

    def home_of(tokens):
        frame = count_floor(tokens, spatial)
        patch = tokens - frame * spatial
        block = count_floor(frame, frames)
        from_side = count_floor(patch, patches)
        inside = (frame - block * frames) * patches + patch - from_side * patches
        return block * spaces + from_side, inside

    token_column = upright(token_row)
    home_row, inside_row = home_of(token_row)
    home_column, inside_column = home_of(token_column)
    earlier = (
        (home_row == home_column) & (inside_row < inside_column) & (token_row >= 0)
    )
    rank = jnp.sum(jnp.where(earlier, 1.0, 0.0), axis=1, keepdims=True)
    wanted = home_column * share + rank
    found = (square_lane.astype(jnp.float32) == wanted) & (token_column >= 0)
    unpermute[...] = jnp.where(found, 1.0, 0.0).astype(jnp.bfloat16)

    for load in loads[:2]:
        load.wait()
    relay(0, 0)
    project(0, 0)
    relay(0, 1)
    project(0, 1)
    relay(1, 1)
    arrive(2, 0)
    project(1, 1)
    relay(1, 0)
    project(1, 0)
    arrive(2, 1)
    relay(2, 0)
    project(2, 0)
    arrive(3, 0)
    relay(2, 1)
    project(2, 1)
    relay(3, 0)
    arrive(3, 1)
    loads[2].wait()
    gather(3, 0)
    make_queries()
    relay(3, 1)
    project(3, 0)
    project(3, 1)
    loads[3].wait()

    def swap_copy(start):
        return remote(
            attended.at[pl.ds(start, rows)], attended_in, swap_sem.at[0], swap_sem.at[1],
            {"clip": partner},
        )

    chunk = rows // 2

    def back_copy(step):
        piece = pl.ds(pl.multiple_of(step * chunk, chunk), chunk)
        return remote(
            made_rows.at[piece], back_rows.at[piece], back_sem.at[0, step], back_sem.at[1, step],
            {"tm": mate, "clip": core_clip(1 - core)},
        )

    def finish(step, carried):
        owner = jnp.where(step == 0, 1 - active_core, active_core)
        start = pl.multiple_of(owner * rows, rows)
        attend_all(start, rows)

        @pl.when(owner != core)
        def _():
            swap_copy(start).start()

        @pl.when(owner == core)
        def _():
            def close(step, carried):
                inside = pl.multiple_of(step * chunk, chunk)
                piece = pl.ds(pl.multiple_of(start + inside, chunk), chunk)
                mine = jnp.dot(
                    attended[piece, :],
                    w_out[pl.ds(pl.multiple_of(core * first_lane, LANES), span), :],
                    preferred_element_type=jnp.float32,
                )

                @pl.when(step == 0)
                def _():
                    swap_copy(start).wait_recv()

                theirs = jnp.dot(
                    attended_in[pl.ds(inside, chunk), :],
                    w_out[pl.ds(pl.multiple_of((1 - core) * first_lane, LANES), span), :],
                    preferred_element_type=jnp.float32,
                )
                hidden = (
                    rows_f32[piece, :] + mine + theirs + b_out_ref[...]
                ).astype(jnp.bfloat16)
                made_rows[pl.ds(inside, chunk), :] = layer_norm(
                    hidden.astype(jnp.float32), final_gain_ref[...], final_shift_ref[...]
                ).astype(jnp.bfloat16)

                @pl.when(idle)
                def _():
                    back_copy(step).start()

                return carried

            lax.fori_loop(0, 2, close, 0)

        return carried

    lax.fori_loop(0, 2, finish, 0)

    def give(source):
        out_ref[0] = jnp.dot(
            unpermute[...], source[...], preferred_element_type=jnp.float32
        ).astype(jnp.bfloat16)

    @pl.when(active)
    def _():
        give(made_rows)

    @pl.when(idle)
    def _():
        for step in range(2):
            back_copy(step).wait_recv()
        give(back_rows)
        for step in range(2):
            back_copy(step).wait_send()

    swap_copy(pl.multiple_of((1 - core) * rows, rows)).wait_send()
    for phase in range(2):
        for half in range(2):
            own_copy(2, line_part[phase], half).wait_send()

            @pl.when(send_across)
            def _():
                own_copy(3, line_part[phase], half).wait_send()

            @pl.when(active)
            def _():
                own_copy(1, near_part[phase], half).wait_send()
                own_copy(0, near_part[phase], half).wait_send()

        for place in range(times):
            part_copy(place, phase, other, 1).wait_send()
            if place:
                part_copy(place, phase, side, 0).wait_send()
                side_copy(place, phase).wait_send()

        @pl.when(inner)
        def _():
            line_copy(phase).wait_send()


def fits_fused(times, spaces, clips, rows, width, owners, capacity):
    all_rows = times * spaces * rows
    held = 2 * (all_rows * width * 3 + width * width * 4 + 6 * rows * width)
    held += 4 * capacity * (width * 6 + all_rows * 6)
    share = capacity // owners
    return (
        spaces == 2
        and times == 4
        and clips % 2 == 0
        and held < VMEM_LIMIT
        and width % LANES == 0
        and HEADS % 2 == 0
        and width // HEADS <= LANES
        and owners == times * spaces
        and share * owners == capacity == rows
        and share % 8 == 0
        and rows % 64 == 0
    )


def fused_local(
    activations,
    attn_gain,
    attn_shift,
    w_qkv,
    b_qkv,
    w_out,
    b_out,
    final_gain,
    final_shift,
    mask_tokens,
    assignment,
):
    frames, patches, width = activations.shape
    rows = frames * patches
    times = lax.axis_size("tm")
    spaces = lax.axis_size("space")
    clips = lax.axis_size("clip")
    owners, capacity = mask_tokens.shape
    if not fits_fused(times, spaces, clips, rows, width, owners, capacity):
        return local(
            activations, attn_gain, attn_shift, w_qkv, b_qkv, w_out, b_out,
            final_gain, final_shift, mask_tokens, assignment,
        )
    half_width = width // 2
    span = width - half_width // LANES * LANES
    quarter = rows // 4
    keys = times * spaces * rows
    vmem = pl.BlockSpec(memory_space=pltpu.VMEM)
    hbm = pl.BlockSpec(memory_space=pl.ANY)
    smem = pl.BlockSpec(memory_space=pltpu.SMEM)
    bf16, f32 = jnp.bfloat16, jnp.float32
    dma = pltpu.SemaphoreType.DMA
    return pl.pallas_call(
        functools.partial(fused_kernel, times, spaces, frames, patches, width // HEADS),
        out_shape=jax.ShapeDtypeStruct((1, capacity, width), bf16),
        in_specs=[vmem, vmem, vmem, hbm, vmem, hbm, vmem, vmem, vmem, vmem, smem],
        out_specs=vmem,
        scratch_shapes=[
            pltpu.VMEM((2, 2, quarter, width), bf16),
            pltpu.VMEM((times, 2, spaces, 2, quarter, width), bf16),
            pltpu.VMEM((keys, span), bf16),
            pltpu.VMEM((keys, span), bf16),
            pltpu.VMEM((width, span), bf16),
            pltpu.VMEM((width, span), bf16),
            pltpu.VMEM((width, span), bf16),
            pltpu.VMEM((width, width), bf16),
            pltpu.VMEM((2 * rows, width), bf16),
            pltpu.VMEM((2 * rows, width), f32),
            pltpu.VMEM((2 * rows, span), bf16),
            pltpu.VMEM((2 * rows, span), f32),
            pltpu.VMEM((2 * rows, span), bf16),
            pltpu.VMEM((rows, span), bf16),
            pltpu.VMEM((rows, width), bf16),
            pltpu.VMEM((rows, width), bf16),
            pltpu.VMEM((rows, rows), bf16),
            pltpu.VMEM((1, 3 * width), f32),
            pltpu.VMEM((5, width), f32),
            dma((4,)),
            dma((4, 2, 2)),
            dma((times, 2, 2)),
            dma((times, 2)),
            dma((2,)),
            dma((times, 2, spaces, 2)),
            dma((2,)),
            dma((2, 2)),
        ],
        compiler_params=pltpu.CompilerParams(
            collective_id=0, has_side_effects=True, vmem_limit_bytes=VMEM_LIMIT
        ),
    )(
        activations.reshape(rows, width),
        attn_gain,
        attn_shift,
        w_qkv,
        b_qkv,
        w_out,
        b_out,
        final_gain,
        final_shift,
        mask_tokens,
        assignment,
    )


def solution(mesh):
    in_specs = (
        P(("clip", "tm"), "space", None),
        P(),
        P(),
        P(),
        P(),
        P(),
        P(),
        P(),
        P(),
        P("clip", None),
        P("clip"),
    )
    out_specs = P(("clip", "tm", "space"), None, None)
    return jax.shard_map(fused_local, mesh=mesh, in_specs=in_specs, out_specs=out_specs, check_vma=False)
```
